32 devices in a mesh: gx: 4 (over y, core), gy: 2 (over x), gz: 4 (over z).
Axes of the slice: x: 2, y: 2, z: 4, core: 2. Of those that a mesh axis runs over, the one named last changes fastest.
Arguments:
- offsets: float32 [4, 2, 8, 3, 128], P('gx', 'gy', 'gz'), may hold values from 0 to 1
- velocity: float32 [4, 2, 8, 3, 128], P('gx', 'gy', 'gz'), may hold values from -6 to 6
- masses: float32 [4, 2, 8, 128], P('gx', 'gy', 'gz'), may hold values from 0.004 to 0.016
- volumes: float32 [4, 2, 8, 128], P('gx', 'gy', 'gz'), may hold values from 0.004 to 0.016
- energies: float32 [4, 2, 8, 128], P('gx', 'gy', 'gz'), may hold values from 0.5 to 2
- smoothing: float32 [4, 2, 8, 128], P('gx', 'gy', 'gz'), may hold values from 0.35 to 0.6
- neighbours: int32 [4, 2, 8, 13], P('gx', 'gy', 'gz'), may hold values from 0 to 25, as said below
- counts: int32 [4, 2, 8], P('gx', 'gy', 'gz'), may hold values from 7 to 13, as said below
Outputs:
- acceleration: float32 [4, 2, 8, 3, 128], P('gx', 'gy', 'gz')
- heating: float32 [4, 2, 8, 128], P('gx', 'gy', 'gz')
The draws below stay inside these ranges and needn't reach their ends.
Inputs may be any that keep to these rules, and one draw needn't show every extreme that they name: `neighbours`: the entries of one leaf are distinct codes. A leaf uses its first counts entries; the leaf at the grid's anchor uses all 13.
All inputs are finite; a program needn't handle non-finite values.
Results may differ from the reference program's by a relative error of at most 0.0003.
Values sent between devices are 32-bit elements; how exact they have to be, the bound alone decides.
No kernel may reach another device: no remote copies, remote signals or barrier semaphores. Data moves between devices by JAX's collectives and lax.ppermute only.
A program may use at most 64 MiB of HBM per device.

```python
import math
import jax
import jax.numpy as jnp
from jax import lax

LX = 1
LY = 1
LZ = 2
P_SIZE = 128
SLOTS = 13
NLX = 4
NLY = 2
NLZ = 8


def draw_neighbours(key, part):
    scores = jax.random.randint(key, (NLX, NLY, NLZ, 26), 0, 1 << 20) * 32 + lax.broadcasted_iota(jnp.int32, (NLX, NLY, NLZ, 26), 3)
    ranked = jnp.argsort(scores, axis=-1)
    return ranked[..., :SLOTS].astype(jnp.int32)


def draw_counts(key, part):
    values = jax.random.randint(jax.random.fold_in(key, 11), (NLX, NLY, NLZ), (SLOTS + 1) // 2, SLOTS + 1)
    return values.at[0, 0, 0].set(SLOTS).astype(jnp.int32)


def shard_levels(own_key, dims, shards, least, top_value):
    factor_of = 1.0
    for axis_at, shards_of in shards:
        steps = jax.random.uniform(jax.random.fold_in(jax.random.fold_in(own_key, 6), axis_at), (shards_of,), jnp.float32, least / len(shards), top_value / len(shards))
        factor_of = factor_of * jnp.repeat(jnp.exp(steps), dims[axis_at] // shards_of).reshape((-1,) + (1,) * (len(dims) - 1 - axis_at))
    return factor_of


def normal_values(own_key, extent, scale, limit, shards=(), held_as=jnp.bfloat16):
    gain = shard_levels(own_key, extent, shards, -0.22, 0.18) if shards else 1.0
    entries = jax.random.normal(own_key, extent, jnp.float32) * scale * gain
    return jnp.minimum(jnp.maximum(entries, -limit), limit).astype(held_as)


def setup_inputs(seed: int = 0) -> dict:
    streams_of = jax.random.split(jax.random.key(seed), 9)
    offsets = jnp.clip(1.0 * jax.random.uniform(streams_of[0], (NLX, NLY, NLZ, 3, P_SIZE), jnp.float32) ** shard_levels(streams_of[0], (NLX, NLY, NLZ, 3, P_SIZE), ((0, 4), (1, 2), (2, 4)), -0.2, 0.2), 0.0, 1.0)
    velocity = normal_values(streams_of[1], (NLX, NLY, NLZ, 3, P_SIZE), 1.0, 6.0, ((0, 4), (1, 2), (2, 4)), jnp.float32)
    masses = jnp.clip(jnp.exp(math.log(0.016) - 1.3862944 * jax.random.uniform(streams_of[2], (NLX, NLY, NLZ, P_SIZE), jnp.float32) ** shard_levels(streams_of[2], (NLX, NLY, NLZ, P_SIZE), ((0, 4), (1, 2), (2, 4)), -0.2, 0.2)), 0.004, 0.016)
    volumes = jnp.clip(jnp.exp(math.log(0.016) - 1.3862944 * jax.random.uniform(streams_of[3], (NLX, NLY, NLZ, P_SIZE), jnp.float32) ** shard_levels(streams_of[3], (NLX, NLY, NLZ, P_SIZE), ((0, 4), (1, 2), (2, 4)), -0.2, 0.2)), 0.004, 0.016)
    energies = jnp.clip(jnp.exp(math.log(2.0) - 1.3862944 * jax.random.uniform(streams_of[4], (NLX, NLY, NLZ, P_SIZE), jnp.float32) ** shard_levels(streams_of[4], (NLX, NLY, NLZ, P_SIZE), ((0, 4), (1, 2), (2, 4)), -0.2, 0.2)), 0.5, 2.0)
    smoothing = jnp.clip(0.35 + 0.25000003 * jax.random.uniform(streams_of[5], (NLX, NLY, NLZ, P_SIZE), jnp.float32) ** shard_levels(streams_of[5], (NLX, NLY, NLZ, P_SIZE), ((0, 4), (1, 2), (2, 4)), -0.2, 0.2), 0.35, 0.6)
    neighbours = draw_neighbours(jax.random.fold_in(streams_of[8], 71), 0)
    counts = draw_counts(jax.random.fold_in(streams_of[8], 71), 0)
    return {"offsets": offsets, "velocity": velocity, "masses": masses, "volumes": volumes, "energies": energies, "smoothing": smoothing, "neighbours": neighbours, "counts": counts}


kernel_norm = 21.0 / (16.0 * math.pi)
pressure_factor = 2.0 / 3.0
ridge_factor = 0.1

def directions(codes):
    shifted = codes + (codes >= 13).astype(jnp.int32)
    return (shifted // 9 - 1, shifted // 3 % 3 - 1, shifted % 3 - 1)

def kernel_parts(left_side, right_side, offset_shift):
    separation = left_side[:, 0:3, :, None] - right_side[:, 0:3, None, :] - offset_shift[:, :, None, None]
    dist_sq = lax.optimization_barrier(jnp.sum(separation * separation, axis=1))
    smooth = 0.5 * (left_side[:, 9, :, None] + right_side[:, 9, None, :])
    inverse = 1.0 / smooth
    q_ratio = jnp.sqrt(dist_sq) * inverse
    remain = jnp.maximum(1.0 - 0.5 * q_ratio, 0.0)
    remain_cubed = remain * remain * remain
    scale_cubed = kernel_norm * inverse ** 3
    kernel_value = scale_cubed * remain_cubed * remain * (2.0 * q_ratio + 1.0)
    kernel_slope = -5.0 * scale_cubed * inverse * inverse * remain_cubed
    return (separation, kernel_value, kernel_slope)

def density_terms(left_side, left_extra, right_side, right_extra, offset_shift):
    separation, kernel_value, kernel_slope = kernel_parts(left_side, right_side, offset_shift)
    with_left = kernel_value * left_side[:, 7, :, None]
    with_right = kernel_value * right_side[:, 7, None, :]
    second_terms = [separation[:, 0] * separation[:, 0], separation[:, 0] * separation[:, 1], separation[:, 0] * separation[:, 2], separation[:, 1] * separation[:, 1], separation[:, 1] * separation[:, 2], separation[:, 2] * separation[:, 2]]
    left_rows = [lax.optimization_barrier(jnp.sum(kernel_value * right_side[:, 6, None, :], axis=2)), lax.optimization_barrier(jnp.sum(with_right, axis=2))]
    left_rows += [lax.optimization_barrier(jnp.sum(with_right * separation[:, column], axis=2)) for column in range(3)]
    left_rows += [lax.optimization_barrier(jnp.sum(with_right * moment_term, axis=2)) for moment_term in second_terms]
    right_rows = [lax.optimization_barrier(jnp.sum(kernel_value * left_side[:, 6, :, None], axis=1)), lax.optimization_barrier(jnp.sum(with_left, axis=1))]
    right_rows += [-lax.optimization_barrier(jnp.sum(with_left * separation[:, column], axis=1)) for column in range(3)]
    right_rows += [lax.optimization_barrier(jnp.sum(with_left * moment_term, axis=1)) for moment_term in second_terms]
    return (jnp.stack(left_rows, axis=1), jnp.stack(right_rows, axis=1))

def corrections(moments, smooth, energy):
    density = moments[..., 0, :]
    zeroth = moments[..., 1, :]
    first_x = moments[..., 2, :]
    first_y = moments[..., 3, :]
    first_z = moments[..., 4, :]
    ridge_term = ridge_factor * smooth * smooth * zeroth
    s_xx = moments[..., 5, :] + ridge_term
    s_xy = moments[..., 6, :]
    s_xz = moments[..., 7, :]
    s_yy = moments[..., 8, :] + ridge_term
    s_yz = moments[..., 9, :]
    s_zz = moments[..., 10, :] + ridge_term
    c_xx = s_yy * s_zz - s_yz * s_yz
    c_xy = s_yz * s_xz - s_xy * s_zz
    c_xz = s_xy * s_yz - s_yy * s_xz
    c_yy = s_xx * s_zz - s_xz * s_xz
    c_yz = s_xy * s_xz - s_xx * s_yz
    c_zz = s_xx * s_yy - s_xy * s_xy
    determinant = s_xx * c_xx + s_xy * c_xy + s_xz * c_xz
    solve_x = (c_xx * first_x + c_xy * first_y + c_xz * first_z) / determinant
    solve_y = (c_xy * first_x + c_yy * first_y + c_yz * first_z) / determinant
    solve_z = (c_xz * first_x + c_yz * first_y + c_zz * first_z) / determinant
    coef_a = 1.0 / (zeroth - (first_x * solve_x + first_y * solve_y + first_z * solve_z))
    pressure = pressure_factor * density * energy
    return jnp.stack([pressure, coef_a, -solve_x, -solve_y, -solve_z], axis=-2)

def force_pair(left_side, left_fields, right_side, right_fields, offset_shift):
    separation, kernel_value, kernel_slope = kernel_parts(left_side, right_side, offset_shift)
    coef_left = left_fields[:, 1, :, None]
    coef_right = right_fields[:, 1, None, :]
    tilt_left = left_fields[:, 2:5, :, None]
    tilt_right = right_fields[:, 2:5, None, :]
    along_left = lax.optimization_barrier(jnp.sum(tilt_left * separation, axis=1))
    along_right = lax.optimization_barrier(jnp.sum(tilt_right * separation, axis=1))
    radial = kernel_slope * (coef_left * (1.0 + along_left) + coef_right * (1.0 - along_right))
    strength = 0.5 * left_side[:, 7, :, None] * right_side[:, 7, None, :] * (left_fields[:, 0, :, None] + right_fields[:, 0, None, :])
    gradient = kernel_value[:, None] * (coef_left[:, None] * tilt_left - coef_right[:, None] * tilt_right) + radial[:, None] * separation
    pair_force = strength[:, None] * gradient
    relative = left_side[:, 3:6, :, None] - right_side[:, 3:6, None, :]
    pair_work = 0.5 * lax.optimization_barrier(jnp.sum(pair_force * relative, axis=1))
    left_sum = jnp.concatenate([-lax.optimization_barrier(jnp.sum(pair_force, axis=3)), lax.optimization_barrier(jnp.sum(pair_work, axis=2))[:, None]], axis=1)
    right_sum = jnp.concatenate([lax.optimization_barrier(jnp.sum(pair_force, axis=2)), lax.optimization_barrier(jnp.sum(pair_work, axis=1))[:, None]], axis=1)
    return (left_sum, right_sum)

def pair_pass(pair_fn, particle_state, extra_state, target, shifts, active, block_size, width):
    leaf_total = particle_state.shape[0]
    per_leaf = particle_state.shape[2]
    slot_count = target.shape[1]
    starts = (jnp.arange(leaf_total // block_size) * block_size).astype(jnp.int32)

    def one_block(start):
        left_side = lax.dynamic_slice_in_dim(particle_state, start, block_size, 0)
        left_extra = lax.dynamic_slice_in_dim(extra_state, start, block_size, 0)
        zero_shift = jnp.zeros((block_size, 3), jnp.float32)
        left_sum = pair_fn(left_side, left_extra, left_side, left_extra, zero_shift)[0]
        right_parts = []
        for slot_index in range(slot_count):
            row_index = lax.dynamic_slice_in_dim(target[:, slot_index], start, block_size, 0)
            right_side = jnp.take(particle_state, row_index, axis=0)
            right_extra = jnp.take(extra_state, row_index, axis=0)
            shift_part = lax.dynamic_slice_in_dim(shifts[:, slot_index], start, block_size, 0)
            scale_part = lax.dynamic_slice_in_dim(active[:, slot_index], start, block_size, 0)[:, None, None]
            one_left, one_right = pair_fn(left_side, left_extra, right_side, right_extra, shift_part)
            left_sum = left_sum + one_left * scale_part
            right_parts.append(one_right * scale_part)
        return (left_sum, jnp.stack(right_parts, axis=1))
    left_all, right_all = lax.map(one_block, starts)
    left_all = left_all.reshape(leaf_total, width, per_leaf)
    right_all = right_all.reshape(leaf_total * slot_count, width, per_leaf)
    return left_all + jnp.zeros_like(left_all).at[target.reshape(-1)].add(right_all)

def reference(offsets, velocity, masses, volumes, energies, smoothing, neighbours, counts):
    grid_x, grid_y, grid_z = (masses.shape[0], masses.shape[1], masses.shape[2])
    per_leaf = masses.shape[3]
    slot_count = neighbours.shape[3]
    leaf_total = grid_x * grid_y * grid_z
    particle_state = jnp.concatenate([offsets, velocity, masses[..., None, :], volumes[..., None, :], energies[..., None, :], smoothing[..., None, :]], axis=-2).reshape(leaf_total, 10, per_leaf)
    coord_x = lax.broadcasted_iota(jnp.int32, (grid_x, grid_y, grid_z), 0).reshape(leaf_total)
    coord_y = lax.broadcasted_iota(jnp.int32, (grid_x, grid_y, grid_z), 1).reshape(leaf_total)
    coord_z = lax.broadcasted_iota(jnp.int32, (grid_x, grid_y, grid_z), 2).reshape(leaf_total)
    step_x, step_y, step_z = directions(neighbours.reshape(leaf_total, slot_count))
    target = (((coord_x[:, None] + step_x) % grid_x * grid_y + (coord_y[:, None] + step_y) % grid_y) * grid_z + (coord_z[:, None] + step_z) % grid_z).astype(jnp.int32)
    shifts = jnp.stack([step_x, step_y, step_z], axis=-1).astype(jnp.float32)
    active = (lax.broadcasted_iota(jnp.int32, (leaf_total, slot_count), 1) < counts.reshape(leaf_total)[:, None]).astype(jnp.float32)
    block_size = LX * LY * LZ
    moments = pair_pass(density_terms, particle_state, particle_state, target, shifts, active, block_size, 11)
    fields = corrections(moments, particle_state[:, 9], particle_state[:, 8])
    pair_sums = pair_pass(force_pair, particle_state, fields, target, shifts, active, block_size, 4)
    mass_flat = particle_state[:, 6]
    acceleration = (pair_sums[:, 0:3] / mass_flat[:, None]).reshape(grid_x, grid_y, grid_z, 3, per_leaf)
    heating = (pair_sums[:, 3] / mass_flat).reshape(grid_x, grid_y, grid_z, per_leaf)
    return (acceleration, heating)
```

```python
import functools
import math

import jax
import jax.numpy as jnp
from jax import lax
from jax.experimental import pallas as pl
from jax.experimental.pallas import tpu as pltpu
from jax.sharding import PartitionSpec as P

kernel_norm = 21.0 / (16.0 * math.pi)
pressure_factor = 2.0 / 3.0
ridge_factor = 0.1
pair_scale = -160.0 * kernel_norm

LIMIT = 16 * 1024 * 1024
AXES = ("gx", "gy", "gz")
X, Y, Z, H, V, M, FLAGS = range(7)
PR, CA, CX, CY, CZ, VX, VY, VZ = range(8)


def code_of(step):
    index = (step[0] + 1) * 9 + (step[1] + 1) * 3 + step[2] + 1
    return index if index < 13 else index - 1


def swap(array, axis, phase):
    count = lax.axis_size(axis)
    pairs = []
    for first in range(phase, count, 2):
        second = (first + 1) % count
        pairs += [(first, second), (second, first)]
    return lax.ppermute(array, axis, pairs)


def swaps(array, axis):
    count = lax.axis_size(axis)
    if count == 2:
        return [swap(array, axis, 0)]
    return [swap(array, axis, 1), swap(array, axis, 0)][::-1]


def beside(get, step, axis):
    if step == 0:
        return get(0)
    if lax.axis_size(axis) == 2:
        return get(1)
    even = lax.axis_index(axis) % 2 == 0
    first, second = (1, 2) if step == 1 else (2, 1)
    return jnp.where(even, get(first), get(second))


def spread(row, per_leaf):
    return jnp.broadcast_to(row, (8, per_leaf))


def block_list(stage, leaves):
    blocks = []
    for dx in (-1, 0, 1):
        for dy in (-1, 0, 1):
            for leaf in range(leaves):
                for dz in (-1, 0, 1):
                    level = leaf + dz
                    if level < 0 or level >= leaves:
                        kind = "z"
                    elif dx:
                        kind = "x"
                    elif dy:
                        kind = "y"
                    else:
                        kind = "own"
                    if kind == stage:
                        blocks.append((leaf, (dx, dy, dz)))
    return blocks


def tile_at(refs, stage, dx, dy, level, leaves):
    def along_x(kx):
        def along_y(ky):
            if stage == "own":
                return refs[0][level]
            if stage == "y":
                return refs[ky - 1][level]
            if stage == "x":
                return refs[kx - 1][ky, level]
            ny = 1 if lax.axis_size("gy") == 2 else 2
            column = kx * (1 + ny) + ky
            even = lax.axis_index("gz") % 2 == 0
            above = level >= leaves
            return jnp.where(
                even, refs[0 if above else 1][column], refs[1 if above else 0][column]
            )

        return beside(along_y, dy, "gy")

    return beside(along_x, dx, "gx")


def tile_key(dx, dy, level):
    if lax.axis_size("gx") == 2:
        dx = abs(dx)
    if lax.axis_size("gy") == 2:
        dy = abs(dy)
    return (dx, dy, level)


def plan(stage, leaves):
    groups = {}
    for number, (leaf, step) in enumerate(block_list(stage, leaves)):
        key = tile_key(step[0], step[1], leaf + step[2])
        groups.setdefault(key, []).append((number, leaf, step))
    return list(groups.items())


def moment_body(stage, leaves, per_leaf, count, *refs):
    own = refs[0]
    sources = refs[1 : 1 + count]
    rest = refs[1 + count :]
    if stage == "own":
        acc_in, rest = None, rest
    else:
        acc_in, rest = rest[0], rest[1:]
    acc_out, vw_out, vg_out, tall_out, row_ref, weight_ref = rest
    if stage == "own":
        sources = (own,)
    groups = plan(stage, leaves)
    for leaf in range(leaves):
        own_tile = own[leaf]
        for part in range(3):
            for shift in (-1, 0, 1):
                row_ref[leaf, 3 * part + shift + 1] = spread(
                    own_tile[part : part + 1] - float(shift), per_leaf
                )
        row_ref[leaf, 9] = spread(own_tile[H : H + 1], per_leaf)
    for place, ((dx, dy, level), blocks) in enumerate(groups):
        tile = tile_at(sources, stage, dx, dy, level, leaves)
        tall_out[place] = tile.T
        for number, leaf, step in blocks:
            if step != (0, 0, 0):
                code = code_of(step)
                weight = (
                    own[leaf][FLAGS : FLAGS + 1, code : code + 1]
                    + tile[FLAGS : FLAGS + 1, 25 - code : 26 - code]
                )
                weight_ref[number] = jnp.broadcast_to(weight, (8, per_leaf))

    def step_fn(strip, carry):
        rows = pl.ds(pl.multiple_of(strip * 8, 8), 8)
        carry = [list(part) for part in carry]
        for place, (_, blocks) in enumerate(groups):

            def column(feature):
                return jnp.broadcast_to(
                    tall_out[place, rows, feature : feature + 1], (8, per_leaf)
                )

            xj, yj, zj, hj, vj, mj = [column(feature) for feature in (X, Y, Z, H, V, M)]
            for number, leaf, step in blocks:
                dx = row_ref[leaf, step[0] + 1] - xj
                dy = row_ref[leaf, step[1] + 4] - yj
                dz = row_ref[leaf, step[2] + 7] - zj
                dist_sq = dx * dx + dy * dy + dz * dz
                inverse = 1.0 / (row_ref[leaf, 9] + hj)
                inverse_sq = inverse * inverse
                dist = dist_sq * lax.rsqrt(jnp.maximum(dist_sq, 1e-30))
                remain = jnp.maximum(1.0 - dist * inverse, 0.0)
                remain_sq = remain * remain
                edge = (inverse_sq * inverse) * (remain_sq * remain)
                if step != (0, 0, 0):
                    edge = edge * weight_ref[number]
                shape = remain * (0.2 * remain - 0.25)
                v_edge = vj * edge
                vw = v_edge * shape
                vg = v_edge * inverse_sq
                vw_out[number, rows, :] = vw
                vg_out[number, rows, :] = vg
                vx, vy, vz = vw * dx, vw * dy, vw * dz
                terms = [
                    (mj * edge) * shape,
                    vw,
                    vx,
                    vy,
                    vz,
                    vx * dx,
                    vx * dy,
                    vx * dz,
                    vy * dy,
                    vy * dz,
                    vz * dz,
                ]
                carry[leaf] = [total + term for total, term in zip(carry[leaf], terms)]
        return tuple(tuple(part) for part in carry)

    if acc_in is None:
        zero = jnp.zeros((8, per_leaf), jnp.float32)
        start = tuple((zero,) * 11 for _ in range(leaves))
    else:
        start = tuple(tuple(acc_in[leaf, k] for k in range(11)) for leaf in range(leaves))
    totals = lax.fori_loop(0, per_leaf // 8, step_fn, start)
    return own, acc_out, totals


def moment_kernel(stage, leaves, per_leaf, count, *refs):
    _, acc_out, totals = moment_body(stage, leaves, per_leaf, count, *refs)
    for leaf in range(leaves):
        for k in range(11):
            acc_out[leaf, k] = totals[leaf][k]


def corrections(moments, smooth, energy):
    density, zeroth, first_x, first_y, first_z, s_xx, s_xy, s_xz, s_yy, s_yz, s_zz = moments
    ridge_term = ridge_factor * smooth * smooth * zeroth
    s_xx = s_xx + ridge_term
    s_yy = s_yy + ridge_term
    s_zz = s_zz + ridge_term
    c_xx = s_yy * s_zz - s_yz * s_yz
    c_xy = s_yz * s_xz - s_xy * s_zz
    c_xz = s_xy * s_yz - s_yy * s_xz
    c_yy = s_xx * s_zz - s_xz * s_xz
    c_yz = s_xy * s_xz - s_xx * s_yz
    c_zz = s_xx * s_yy - s_xy * s_xy
    determinant = s_xx * c_xx + s_xy * c_xy + s_xz * c_xz
    solve_x = (c_xx * first_x + c_xy * first_y + c_xz * first_z) / determinant
    solve_y = (c_xy * first_x + c_yy * first_y + c_yz * first_z) / determinant
    solve_z = (c_xz * first_x + c_yz * first_y + c_zz * first_z) / determinant
    coef_a = 1.0 / (zeroth - (first_x * solve_x + first_y * solve_y + first_z * solve_z))
    pressure = pressure_factor * density * energy
    return [pressure, coef_a, -coef_a * solve_x, -coef_a * solve_y, -coef_a * solve_z]


def field_kernel(leaves, per_leaf, count, *refs):
    velocity, energies, fields_out = refs[-8:-5]
    own, _, totals = moment_body(
        "z", leaves, per_leaf, count, *refs[: 2 + count], None, *refs[-5:]
    )
    rows = []
    for k in range(11):
        parts = [jnp.sum(totals[leaf][k], axis=0, keepdims=True) for leaf in range(leaves)]
        rows.append(jnp.concatenate(parts, axis=0))
    smooth = jnp.concatenate([own[leaf][H : H + 1] for leaf in range(leaves)], axis=0)
    fields = corrections(rows, smooth, energies[0, 0])
    for k, value in enumerate(fields):
        for leaf in range(leaves):
            fields_out[leaf, k : k + 1, :] = value[leaf : leaf + 1]
    for leaf in range(leaves):
        fields_out[leaf, VX : VZ + 1, :] = velocity[0, 0, leaf]


def force_body(stage, leaves, per_leaf, count, *refs):
    own, own_fields = refs[0], refs[1]
    sources = refs[2 : 2 + count]
    rest = refs[2 + count :]
    if stage == "own":
        acc_in = None
        sources = (own_fields,)
    else:
        acc_in, rest = rest[0], rest[1:]
    vw_in, vg_in, tall_in = rest[:3]
    tall_ref, row_ref = rest[-2:]
    groups = plan(stage, leaves)
    for leaf in range(leaves):
        own_tile = own[leaf]
        own_field = own_fields[leaf]
        for part in range(3):
            for shift in (-1, 0, 1):
                row_ref[leaf, 3 * part + shift + 1] = spread(
                    own_tile[part : part + 1] - float(shift), per_leaf
                )
        for k in range(5):
            row_ref[leaf, 9 + k] = spread(own_field[k : k + 1], per_leaf)
    for place, ((dx, dy, level), blocks) in enumerate(groups):
        tall_ref[place] = tile_at(sources, stage, dx, dy, level, leaves).T

    def step_fn(strip, carry):
        rows = pl.ds(pl.multiple_of(strip * 8, 8), 8)
        carry = [list(part) for part in carry]
        for place, (_, blocks) in enumerate(groups):

            def column(ref, feature):
                return jnp.broadcast_to(ref[place, rows, feature : feature + 1], (8, per_leaf))

            xj, yj, zj = [column(tall_in, feature) for feature in (X, Y, Z)]
            pj, aj, cxj, cyj, czj, vxj, vyj, vzj = [column(tall_ref, k) for k in range(8)]
            for number, leaf, step in blocks:
                dx = row_ref[leaf, step[0] + 1] - xj
                dy = row_ref[leaf, step[1] + 4] - yj
                dz = row_ref[leaf, step[2] + 7] - zj
                tx = row_ref[leaf, 11] - cxj
                ty = row_ref[leaf, 12] - cyj
                tz = row_ref[leaf, 13] - czj
                strength = row_ref[leaf, 9] + pj
                along = tx * dx + ty * dy + tz * dz
                flat = strength * vw_in[number, rows, :]
                radial = (strength * vg_in[number, rows, :]) * ((row_ref[leaf, 10] + aj) + along)
                fx = flat * tx + radial * dx
                fy = flat * ty + radial * dy
                fz = flat * tz + radial * dz
                work = fx * vxj + fy * vyj + fz * vzj
                carry[leaf] = [
                    total + term for total, term in zip(carry[leaf], [fx, fy, fz, work])
                ]
        return tuple(tuple(part) for part in carry)

    if acc_in is None:
        zero = jnp.zeros((8, per_leaf), jnp.float32)
        start = tuple((zero,) * 4 for _ in range(leaves))
    else:
        start = tuple(tuple(acc_in[leaf, k] for k in range(4)) for leaf in range(leaves))
    return lax.fori_loop(0, per_leaf // 8, step_fn, start)


def force_kernel(stage, leaves, per_leaf, count, *refs):
    totals = force_body(stage, leaves, per_leaf, count, *refs)
    acc_out = refs[-3]
    for leaf in range(leaves):
        for k in range(4):
            acc_out[leaf, k] = totals[leaf][k]


def finish_kernel(leaves, per_leaf, count, *refs):
    totals = force_body("z", leaves, per_leaf, count, *refs)
    own, own_fields = refs[0], refs[1]
    acceleration, heating = refs[-4], refs[-3]
    for leaf in range(leaves):
        tile, field = own[leaf], own_fields[leaf]
        ratio = tile[V : V + 1] / tile[M : M + 1]
        force = [jnp.sum(totals[leaf][k], axis=0, keepdims=True) for k in range(4)]
        work = -force[3]
        for k in range(3):
            acceleration[0, 0, leaf, k : k + 1, :] = (-0.5 * ratio) * force[k]
            work = work + field[VX + k : VX + k + 1] * force[k]
        heating[0, 0, leaf : leaf + 1, :] = (0.25 * ratio) * work


def pack_kernel(leaves, per_leaf, offsets, volumes, masses, smoothing, neighbours, counts, out):
    lane = lax.broadcasted_iota(jnp.int32, (1, per_leaf), 1)
    for leaf in range(leaves):
        flags = jnp.zeros((1, per_leaf), jnp.float32)
        for slot in range(neighbours.shape[3]):
            code = jnp.where(slot < counts[0, 0, leaf], neighbours[0, 0, leaf, slot], -1)
            flags = flags + jnp.where(lane == code, 1.0, 0.0)
        out[leaf, X : Z + 1, :] = offsets[0, 0, leaf]
        out[leaf, H : H + 1, :] = smoothing[0, 0, leaf : leaf + 1]
        out[leaf, V : V + 1, :] = pair_scale * volumes[0, 0, leaf : leaf + 1]
        out[leaf, M : M + 1, :] = pair_scale * masses[0, 0, leaf : leaf + 1]
        out[leaf, FLAGS : FLAGS + 1, :] = flags
        out[leaf, FLAGS + 1 : FLAGS + 2, :] = jnp.zeros((1, per_leaf), jnp.float32)


def per_device(offsets, velocity, masses, volumes, energies, smoothing, neighbours, counts):
    leaves, per_leaf = masses.shape[2], masses.shape[3]
    f32 = jnp.float32
    vmem = pl.BlockSpec(memory_space=pltpu.VMEM)
    smem = pl.BlockSpec(memory_space=pltpu.SMEM)
    params = pltpu.CompilerParams(vmem_limit_bytes=LIMIT)
    parity = lax.axis_index("gz") % 2 == 0

    def cost(blocks, ops):
        return pl.CostEstimate(
            flops=blocks * per_leaf * per_leaf * ops, bytes_accessed=blocks * 4096, transcendentals=0
        )

    own = pl.pallas_call(
        functools.partial(pack_kernel, leaves, per_leaf),
        out_shape=jax.ShapeDtypeStruct((leaves, 8, per_leaf), f32),
        in_specs=[vmem] * 4 + [smem] * 2,
        out_specs=vmem,
        compiler_params=params,
        name="pack",
    )(offsets, volumes, masses, smoothing, neighbours, counts)

    def exchange_y(tile):
        return swaps(tile, "gy")

    def exchange_x(tile, from_y):
        return swaps(jnp.stack([tile] + from_y, axis=0), "gx")

    def exchange_z(tile, from_y, from_x):
        column = jnp.concatenate([jnp.stack([tile] + from_y, axis=0)] + from_x, axis=0)
        bottom, top = column[:, 0], column[:, leaves - 1]
        far = swap(jnp.where(parity, bottom, top), "gz", 1)
        near = swap(jnp.where(parity, top, bottom), "gz", 0)
        return [near, far]

    stages = ("own", "y", "x", "z")
    sizes = {stage: len(block_list(stage, leaves)) for stage in stages}
    tiles = {stage: len(plan(stage, leaves)) for stage in stages}

    def moment_call(stage, sources, acc):
        size = sizes[stage]
        kept = [
            jax.ShapeDtypeStruct((size, per_leaf, per_leaf), f32),
            jax.ShapeDtypeStruct((size, per_leaf, per_leaf), f32),
            jax.ShapeDtypeStruct((tiles[stage], per_leaf, 8), f32),
        ]
        operands = [own] + list(sources) + ([] if acc is None else [acc])
        if stage == "z":
            body = functools.partial(field_kernel, leaves, per_leaf, len(sources))
            operands += [velocity, energies]
            first = jax.ShapeDtypeStruct((leaves, 8, per_leaf), f32)
        else:
            body = functools.partial(moment_kernel, stage, leaves, per_leaf, len(sources))
            first = jax.ShapeDtypeStruct((leaves, 11, 8, per_leaf), f32)
        scratch = [
            pltpu.VMEM((leaves, 10, 8, per_leaf), f32),
            pltpu.VMEM((size, 8, per_leaf), f32),
        ]
        return pl.pallas_call(
            body,
            out_shape=[first] + kept,
            in_specs=[vmem] * len(operands),
            out_specs=[vmem] * 4,
            scratch_shapes=scratch,
            compiler_params=params,
            cost_estimate=cost(size, 55),
            name="moments_" + stage,
        )(*operands)

    def force_call(stage, sources, acc, kept, fields):
        size = sizes[stage]
        operands = [own, fields] + list(sources) + ([] if acc is None else [acc]) + list(kept)
        if stage == "z":
            body = functools.partial(finish_kernel, leaves, per_leaf, len(sources))
            out = [
                jax.ShapeDtypeStruct((1, 1, leaves, 3, per_leaf), f32),
                jax.ShapeDtypeStruct((1, 1, leaves, per_leaf), f32),
            ]
        else:
            body = functools.partial(force_kernel, stage, leaves, per_leaf, len(sources))
            out = [jax.ShapeDtypeStruct((leaves, 4, 8, per_leaf), f32)]
        scratch = [
            pltpu.VMEM((tiles[stage], per_leaf, 8), f32),
            pltpu.VMEM((leaves, 14, 8, per_leaf), f32),
        ]
        return pl.pallas_call(
            body,
            out_shape=out,
            in_specs=[vmem] * len(operands),
            out_specs=[vmem] * len(out),
            scratch_shapes=scratch,
            compiler_params=params,
            cost_estimate=cost(size, 36),
            name="force_" + stage,
        )(*operands)

    from_y = exchange_y(own)
    acc, *kept_own = moment_call("own", [], None)
    from_x = exchange_x(own, from_y)
    acc, *kept_y = moment_call("y", from_y, acc)
    from_z = exchange_z(own, from_y, from_x)
    acc, *kept_x = moment_call("x", from_x, acc)
    fields, *kept_z = moment_call("z", from_z, acc)

    field_y = exchange_y(fields)
    (acc,) = force_call("own", [], None, kept_own, fields)
    field_x = exchange_x(fields, field_y)
    (acc,) = force_call("y", field_y, acc, kept_y, fields)
    field_z = exchange_z(fields, field_y, field_x)
    (acc,) = force_call("x", field_x, acc, kept_x, fields)
    acceleration, heating = force_call("z", field_z, acc, kept_z, fields)
    return (acceleration, heating)


def solution(mesh):
    in_specs = (
        P("gx", "gy", "gz", None, None),
        P("gx", "gy", "gz", None, None),
        P("gx", "gy", "gz", None),
        P("gx", "gy", "gz", None),
        P("gx", "gy", "gz", None),
        P("gx", "gy", "gz", None),
        P("gx", "gy", "gz", None),
        P("gx", "gy", "gz"),
    )
    out_specs = (P("gx", "gy", "gz", None, None), P("gx", "gy", "gz", None))
    return jax.shard_map(
        per_device, mesh=mesh, in_specs=in_specs, out_specs=out_specs, check_vma=False
    )
```

```python
import functools
import math

import jax
import jax.numpy as jnp
from jax import lax
from jax.experimental import pallas as pl
from jax.experimental.pallas import tpu as pltpu
from jax.sharding import PartitionSpec as P

kernel_norm = 21.0 / (16.0 * math.pi)
pressure_factor = 2.0 / 3.0
ridge_factor = 0.1
pair_scale = -160.0 * kernel_norm

LIMIT = 16 * 1024 * 1024
AXES = ("gx", "gy", "gz")
X, Y, Z, H, V, M, FLAGS = range(7)
PR, CA, CX, CY, CZ, VX, VY, VZ = range(8)


def code_of(step):
    index = (step[0] + 1) * 9 + (step[1] + 1) * 3 + step[2] + 1
    return index if index < 13 else index - 1


def swap(array, axis, phase):
    count = lax.axis_size(axis)
    pairs = []
    for first in range(phase, count, 2):
        second = (first + 1) % count
        pairs += [(first, second), (second, first)]
    return lax.ppermute(array, axis, pairs)


def swaps(array, axis):
    count = lax.axis_size(axis)
    if count == 2:
        return [swap(array, axis, 0)]
    return [swap(array, axis, 1), swap(array, axis, 0)][::-1]


def beside(get, step, axis):
    if step == 0:
        return get(0)
    if lax.axis_size(axis) == 2:
        return get(1)
    even = lax.axis_index(axis) % 2 == 0
    first, second = (1, 2) if step == 1 else (2, 1)
    return jnp.where(even, get(first), get(second))


def split(values, parts):
    pieces = []
    for _ in range(parts - 1):
        piece = values.astype(jnp.bfloat16).astype(jnp.float32)
        pieces.append(piece)
        values = values - piece
    return pieces + [values]


def stacked(parts):
    return jnp.concatenate(parts, axis=0).astype(jnp.bfloat16)


def left_form(features):
    high, middle, low = split(features, 3)
    return stacked([high, high, middle, high, low, middle]).T


def right_form(features):
    high, middle, low = split(features, 3)
    return stacked([high, middle, high, low, high, middle])


def pair_matrix(features):
    return jnp.concatenate(split(features, 2), axis=0).astype(jnp.bfloat16)


def feature_rows(features):
    rows = stacked(split(features, 3))
    return jnp.concatenate([rows, rows], axis=1)


def dot(left, right):
    return jnp.dot(left, right, preferred_element_type=jnp.float32)


def rows_of(tile, first, count=1):
    return [tile[k : k + 1] for k in range(first, first + count)]


def block_list(stage, leaves):
    blocks = []
    for dx in (-1, 0, 1):
        for dy in (-1, 0, 1):
            for leaf in range(leaves):
                for dz in (-1, 0, 1):
                    level = leaf + dz
                    if level < 0 or level >= leaves:
                        kind = "z"
                    elif dx:
                        kind = "x"
                    elif dy:
                        kind = "y"
                    else:
                        kind = "own"
                    if kind == stage:
                        blocks.append((leaf, (dx, dy, dz)))
    return blocks


def tile_at(refs, stage, dx, dy, level, leaves):
    def along_x(kx):
        def along_y(ky):
            if stage == "own":
                return refs[0][level]
            if stage == "y":
                return refs[ky - 1][level]
            if stage == "x":
                return refs[kx - 1][ky, level]
            ny = 1 if lax.axis_size("gy") == 2 else 2
            column = kx * (1 + ny) + ky
            even = lax.axis_index("gz") % 2 == 0
            above = level >= leaves
            return jnp.where(
                even, refs[0 if above else 1][column], refs[1 if above else 0][column]
            )

        return beside(along_y, dy, "gy")

    return beside(along_x, dx, "gx")


def tile_key(dx, dy, level):
    if lax.axis_size("gx") == 2:
        dx = abs(dx)
    if lax.axis_size("gy") == 2:
        dy = abs(dy)
    return (dx, dy, level)


def plan(stage, leaves):
    groups = {}
    for number, (leaf, step) in enumerate(block_list(stage, leaves)):
        key = tile_key(step[0], step[1], leaf + step[2])
        groups.setdefault(key, []).append((number, leaf, step))
    return list(groups.items())


def level_centre(level, leaves):
    return float(level) - 0.5 * (leaves - 1)


def pair_weight(own_tile, tile, step):
    if step == (0, 0, 0):
        return None
    code = code_of(step)
    weight = own_tile[FLAGS : FLAGS + 1, code : code + 1] + tile[FLAGS : FLAGS + 1, 25 - code : 26 - code]
    return jnp.broadcast_to(weight, (48, tile.shape[1]))


def add_weighted(acc, leaf, sums, weight):
    acc[leaf] = acc[leaf] + (sums if weight is None else sums * weight)


def place_rows(tile, dx, dy, level, leaves):
    centre = (float(dx), float(dy), level_centre(level, leaves))
    return [row + (part - 0.5) for row, part in zip(rows_of(tile, X, 3), centre)]


def moment_features(tile, dx, dy, level, leaves):
    x, y, z = place_rows(tile, dx, dy, level, leaves)
    (v, m) = rows_of(tile, V, 2)
    vx, vy, vz = v * x, v * y, v * z
    rows = [v, vx, vy, vz, vx * x, vx * y, vx * z, vy * y, vy * z, vz * z, m]
    return feature_rows(jnp.concatenate(rows + [jnp.zeros_like(v)] * 5, axis=0))


def moment_body(stage, leaves, per_leaf, own, sources, acc, w_out, g_out):
    one = jnp.ones((1, per_leaf), jnp.float32)
    zero = jnp.zeros((1, per_leaf), jnp.float32)
    number = 0
    widths = {}
    for leaf in range(leaves):
        smooth = rows_of(own[leaf], H)[0]
        widths[leaf] = right_form(
            jnp.concatenate([zero, smooth, zero, zero, zero, one, zero, zero], axis=0)
        )
    for (dx, dy, level), blocks in plan(stage, leaves):
        tile = tile_at(sources, stage, dx, dy, level, leaves)
        xj, yj, zj = [row - 0.5 for row in rows_of(tile, X, 3)]
        near = xj * xj + yj * yj + zj * zj
        left = left_form(
            jnp.concatenate([near, one, xj, yj, zj, tile[H : H + 1], zero, zero], axis=0)
        )
        inverses = {}
        features = {}
        for number, leaf, step in blocks:
            if leaf not in inverses:
                inverses[leaf] = 1.0 / dot(left, widths[leaf])
            if step[:2] not in features:
                features[step[:2]] = moment_features(tile, step[0], step[1], level, leaves)
            xi, yi, zi = [
                row - (0.5 + shift) for row, shift in zip(rows_of(own[leaf], X, 3), step)
            ]
            far = xi * xi + yi * yi + zi * zi
            right = right_form(
                jnp.concatenate(
                    [one, far, -2.0 * xi, -2.0 * yi, -2.0 * zi, zero, zero, zero], axis=0
                )
            )
            inverse = inverses[leaf]
            inverse_sq = inverse * inverse
            dist_sq = jnp.maximum(dot(left, right), 1e-30)
            dist = dist_sq * lax.rsqrt(dist_sq)
            remain = jnp.maximum(1.0 - dist * inverse, 0.0)
            edge = (inverse_sq * inverse) * (remain * remain * remain)
            pair_w = pair_matrix(edge * (remain * (0.2 * remain - 0.25)))
            w_out[number] = pair_w
            g_out[number] = edge * inverse_sq
            weight = pair_weight(own[leaf], tile, step)
            add_weighted(acc, leaf, dot(features[step[:2]], pair_w), weight)


def moment_kernel(stage, leaves, per_leaf, count, *refs):
    own = refs[0]
    sources = refs[1 : 1 + count] if count else (own,)
    rest = refs[1 + count :]
    if stage == "own":
        acc, w_out, g_out = rest
        acc[...] = jnp.zeros_like(acc)
    else:
        acc_in, acc, w_out, g_out = rest
        acc[...] = acc_in[...]
    moment_body(stage, leaves, per_leaf, own, sources, acc, w_out, g_out)


def corrections(moments, smooth, energy):
    density, zeroth, first_x, first_y, first_z, s_xx, s_xy, s_xz, s_yy, s_yz, s_zz = moments
    ridge_term = ridge_factor * smooth * smooth * zeroth
    s_xx = s_xx + ridge_term
    s_yy = s_yy + ridge_term
    s_zz = s_zz + ridge_term
    c_xx = s_yy * s_zz - s_yz * s_yz
    c_xy = s_yz * s_xz - s_xy * s_zz
    c_xz = s_xy * s_yz - s_yy * s_xz
    c_yy = s_xx * s_zz - s_xz * s_xz
    c_yz = s_xy * s_xz - s_xx * s_yz
    c_zz = s_xx * s_yy - s_xy * s_xy
    determinant = s_xx * c_xx + s_xy * c_xy + s_xz * c_xz
    solve_x = (c_xx * first_x + c_xy * first_y + c_xz * first_z) / determinant
    solve_y = (c_xy * first_x + c_yy * first_y + c_yz * first_z) / determinant
    solve_z = (c_xz * first_x + c_yz * first_y + c_zz * first_z) / determinant
    coef_a = 1.0 / (zeroth - (first_x * solve_x + first_y * solve_y + first_z * solve_z))
    pressure = pressure_factor * density * energy
    return [pressure, coef_a, -coef_a * solve_x, -coef_a * solve_y, -coef_a * solve_z]

def gathered(acc, leaf):
    sums = acc[leaf]
    return sums[0:16] + (sums[16:32] + sums[32:48])


def field_kernel(leaves, per_leaf, count, *refs):
    own = refs[0]
    sources = refs[1 : 1 + count]
    acc_in, extra, fields_out, w_out, g_out, acc = refs[1 + count :]
    acc[...] = acc_in[...]
    moment_body("z", leaves, per_leaf, own, sources, acc, w_out, g_out)
    columns = []
    for leaf in range(leaves):
        sums = gathered(acc, leaf)
        zeroth, fx, fy, fz, sxx, sxy, sxz, syy, syz, szz, density = rows_of(sums, 0, 11)
        x, y, z = place_rows(own[leaf], 0, 0, leaf, leaves)
        mx, my, mz = x * zeroth - fx, y * zeroth - fy, z * zeroth - fz
        columns.append(
            [
                density,
                zeroth,
                mx,
                my,
                mz,
                x * mx - x * fx + sxx,
                x * my - y * fx + sxy,
                x * mz - z * fx + sxz,
                y * my - y * fy + syy,
                y * mz - z * fy + syz,
                z * mz - z * fz + szz,
                own[leaf][H : H + 1],
                extra[leaf][3:4],
            ]
        )
    rows = [jnp.concatenate(parts, axis=0) for parts in zip(*columns)]
    fields = corrections(rows[:11], rows[11], rows[12])
    for leaf in range(leaves):
        for k, value in enumerate(fields):
            fields_out[leaf, k : k + 1, :] = value[leaf : leaf + 1]
        fields_out[leaf, VX : VZ + 1, :] = extra[leaf][0:3]


def force_body(stage, leaves, per_leaf, own, fields, sources, places, accs, w_in, g_in):
    one = jnp.ones((1, per_leaf), jnp.float32)
    acc_w, acc_g = accs
    for (dx, dy, level), blocks in plan(stage, leaves):
        tile = tile_at(places, stage, dx, dy, level, leaves)
        field = tile_at(sources, stage, dx, dy, level, leaves)
        xj, yj, zj = [row - 0.5 for row in rows_of(tile, X, 3)]
        pressure, coef, cx, cy, cz, vx, vy, vz = rows_of(field, 0, 8)
        volume = tile[V : V + 1]
        left = left_form(
            jnp.concatenate(
                [one, coef + (cx * xj + cy * yj + cz * zj), xj, yj, zj, cx, cy, cz], axis=0
            )
        )

        def weighted(a, b, c):
            first = volume * jnp.concatenate(
                [one, a, b, c, vx, vy, vz, a * vx + b * vy + c * vz], axis=0
            )
            return feature_rows(jnp.concatenate([first, pressure * first], axis=0))

        with_w = weighted(cx, cy, cz)
        with_g = {}
        for number, leaf, step in blocks:
            if step[:2] not in with_g:
                with_g[step[:2]] = weighted(*place_rows(tile, step[0], step[1], level, leaves))
            xi, yi, zi = [
                row - (0.5 + shift) for row, shift in zip(rows_of(own[leaf], X, 3), step)
            ]
            _, coef_i, cxi, cyi, czi = rows_of(fields[leaf], 0, 5)
            right = right_form(
                jnp.concatenate(
                    [coef_i + (cxi * xi + cyi * yi + czi * zi), one]
                    + [-cxi, -cyi, -czi, -xi, -yi, -zi],
                    axis=0,
                )
            )
            radial = pair_matrix(g_in[number] * dot(left, right))
            weight = pair_weight(own[leaf], tile, step)
            add_weighted(acc_w, leaf, dot(with_w, w_in[number]), weight)
            add_weighted(acc_g, leaf, dot(with_g[step[:2]], radial), weight)


def force_setup(stage, count, refs):
    own, fields = refs[0], refs[1]
    sources = refs[2 : 2 + count] if count else (fields,)
    places = refs[2 + count : 2 + 2 * count] if count else (own,)
    return own, fields, sources, places, refs[2 + 2 * count :]


def force_kernel(stage, leaves, per_leaf, count, *refs):
    own, fields, sources, places, rest = force_setup(stage, count, refs)
    if stage == "own":
        w_in, g_in, acc_w, acc_g = rest
        acc_w[...] = jnp.zeros_like(acc_w)
        acc_g[...] = jnp.zeros_like(acc_g)
    else:
        w_before, g_before, w_in, g_in, acc_w, acc_g = rest
        acc_w[...] = w_before[...]
        acc_g[...] = g_before[...]
    force_body(
        stage, leaves, per_leaf, own, fields, sources, places, (acc_w, acc_g), w_in, g_in
    )


def finish_kernel(leaves, per_leaf, count, *refs):
    own, fields, sources, places, rest = force_setup("z", count, refs)
    w_before, g_before, w_in, g_in, acceleration, heating, acc_w, acc_g = rest
    acc_w[...] = w_before[...]
    acc_g[...] = g_before[...]
    force_body(
        "z", leaves, per_leaf, own, fields, sources, places, (acc_w, acc_g), w_in, g_in
    )
    for leaf in range(leaves):
        tile = own[leaf]
        pressure, _, cx, cy, cz, vx, vy, vz = rows_of(fields[leaf], 0, 8)
        sums_w, sums_g = gathered(acc_w, leaf), gathered(acc_g, leaf)
        both_w = pressure * sums_w[0:8] + sums_w[8:16]
        both_g = pressure * sums_g[0:8] + sums_g[8:16]
        w_rows, g_rows = rows_of(both_w, 0, 8), rows_of(both_g, 0, 8)
        coefs = (cx, cy, cz)
        spots = place_rows(tile, 0, 0, leaf, leaves)
        ratio = tile[V : V + 1] / tile[M : M + 1]
        work = w_rows[7] + g_rows[7]
        for k, (coef, spot, speed) in enumerate(zip(coefs, spots, (vx, vy, vz))):
            force = (coef * w_rows[0] - w_rows[1 + k]) + (spot * g_rows[0] - g_rows[1 + k])
            work = work + speed * force - coef * w_rows[4 + k] - spot * g_rows[4 + k]
            acceleration[0, 0, k, leaf : leaf + 1, :] = (-0.5 * ratio) * force
        heating[0, 0, leaf : leaf + 1, :] = (0.25 * ratio) * work


def pack_kernel(leaves, per_leaf, *refs):
    inputs = refs[:6]
    neighbours, counts = refs[6:8]
    out, extra = refs[8:10]
    held = refs[10:16]
    sems = refs[16]
    copies = [
        pltpu.make_async_copy(source, target, sems.at[k])
        for k, (source, target) in enumerate(zip(inputs, held))
    ]
    for copy in copies:
        copy.start()
    lane = lax.broadcasted_iota(jnp.int32, (1, per_leaf), 1)
    for leaf in range(leaves):
        flags = jnp.zeros((1, per_leaf), jnp.float32)
        for slot in range(neighbours.shape[3]):
            code = jnp.where(slot < counts[0, 0, leaf], neighbours[0, 0, leaf, slot], -1)
            flags = flags + jnp.where(lane == code, 1.0, 0.0)
        out[leaf, FLAGS : FLAGS + 1, :] = flags
        out[leaf, FLAGS + 1 : FLAGS + 2, :] = jnp.zeros((1, per_leaf), jnp.float32)
        extra[leaf, 4:8, :] = jnp.zeros((4, per_leaf), jnp.float32)
    for copy in copies:
        copy.wait()
    offsets, velocity, masses, volumes, energies, smoothing = held
    for leaf in range(leaves):
        one = slice(leaf, leaf + 1)
        for part in range(3):
            out[leaf, part : part + 1, :] = offsets[0, 0, part, one]
            extra[leaf, part : part + 1, :] = velocity[0, 0, part, one]
        out[leaf, H : H + 1, :] = smoothing[0, 0, one]
        out[leaf, V : V + 1, :] = pair_scale * volumes[0, 0, one]
        out[leaf, M : M + 1, :] = pair_scale * masses[0, 0, one]
        extra[leaf, 3:4, :] = energies[0, 0, one]


def per_device(offsets, velocity, masses, volumes, energies, smoothing, neighbours, counts):
    leaves, per_leaf = masses.shape[2], masses.shape[3]
    f32, bf16 = jnp.float32, jnp.bfloat16
    vmem = pl.BlockSpec(memory_space=pltpu.VMEM)
    smem = pl.BlockSpec(memory_space=pltpu.SMEM)
    anywhere = pl.BlockSpec(memory_space=pl.ANY)
    params = pltpu.CompilerParams(vmem_limit_bytes=LIMIT)
    parity = lax.axis_index("gz") % 2 == 0
    offsets = jnp.swapaxes(offsets, 2, 3)
    velocity = jnp.swapaxes(velocity, 2, 3)

    def cost(blocks, ops):
        return pl.CostEstimate(
            flops=blocks * per_leaf * per_leaf * ops, bytes_accessed=blocks * 4096, transcendentals=0
        )

    inputs = (offsets, velocity, masses, volumes, energies, smoothing)
    own, extra = pl.pallas_call(
        functools.partial(pack_kernel, leaves, per_leaf),
        out_shape=[jax.ShapeDtypeStruct((leaves, 8, per_leaf), f32)] * 2,
        in_specs=[anywhere] * 6 + [smem] * 2,
        out_specs=[vmem] * 2,
        scratch_shapes=[pltpu.VMEM(array.shape, f32) for array in inputs]
        + [pltpu.SemaphoreType.DMA((6,))],
        compiler_params=params,
        name="pack",
    )(*inputs, neighbours, counts)

    def exchange_y(tile):
        return swaps(tile, "gy")

    def exchange_x(tile, from_y):
        return swaps(jnp.stack([tile] + from_y, axis=0), "gx")

    def exchange_z(tile, from_y, from_x):
        column = jnp.concatenate([jnp.stack([tile] + from_y, axis=0)] + from_x, axis=0)
        bottom, top = column[:, 0], column[:, leaves - 1]
        far = swap(jnp.where(parity, bottom, top), "gz", 1)
        near = swap(jnp.where(parity, top, bottom), "gz", 0)
        return [near, far]

    stages = ("own", "y", "x", "z")
    sizes = {stage: len(block_list(stage, leaves)) for stage in stages}
    acc_shape = jax.ShapeDtypeStruct((leaves, 48, per_leaf), f32)
    acc_scratch = pltpu.VMEM((leaves, 48, per_leaf), f32)

    def moment_call(stage, sources, acc):
        size = sizes[stage]
        kept = [
            jax.ShapeDtypeStruct((size, 2 * per_leaf, per_leaf), bf16),
            jax.ShapeDtypeStruct((size, per_leaf, per_leaf), f32),
        ]
        operands = [own] + list(sources) + ([] if acc is None else [acc])
        scratch = []
        if stage == "z":
            body = functools.partial(field_kernel, leaves, per_leaf, len(sources))
            operands += [extra]
            first = jax.ShapeDtypeStruct((leaves, 8, per_leaf), f32)
            scratch = [acc_scratch]
        else:
            body = functools.partial(moment_kernel, stage, leaves, per_leaf, len(sources))
            first = acc_shape
        return pl.pallas_call(
            body,
            out_shape=[first] + kept,
            in_specs=[vmem] * len(operands),
            out_specs=[vmem] * 3,
            scratch_shapes=scratch,
            compiler_params=params,
            cost_estimate=cost(size, 55),
            name="moments_" + stage,
        )(*operands)

    def force_call(stage, sources, places, accs, kept, fields):
        size = sizes[stage]
        operands = [own, fields] + list(sources) + list(places) + list(accs) + list(kept)
        scratch = []
        if stage == "z":
            body = functools.partial(finish_kernel, leaves, per_leaf, len(sources))
            out = [
                jax.ShapeDtypeStruct((1, 1, 3, leaves, per_leaf), f32),
                jax.ShapeDtypeStruct((1, 1, leaves, per_leaf), f32),
            ]
            scratch = [acc_scratch] * 2
        else:
            body = functools.partial(force_kernel, stage, leaves, per_leaf, len(sources))
            out = [acc_shape] * 2
        return pl.pallas_call(
            body,
            out_shape=out,
            in_specs=[vmem] * len(operands),
            out_specs=[vmem] * len(out),
            scratch_shapes=scratch,
            compiler_params=params,
            cost_estimate=cost(size, 36),
            name="force_" + stage,
        )(*operands)

    from_y = exchange_y(own)
    acc, *kept_own = moment_call("own", [], None)
    from_x = exchange_x(own, from_y)
    acc, *kept_y = moment_call("y", from_y, acc)
    from_z = exchange_z(own, from_y, from_x)
    acc, *kept_x = moment_call("x", from_x, acc)
    fields, *kept_z = moment_call("z", from_z, acc)

    field_y = exchange_y(fields)
    accs = force_call("own", [], [], [], kept_own, fields)
    field_x = exchange_x(fields, field_y)
    accs = force_call("y", field_y, from_y, accs, kept_y, fields)
    field_z = exchange_z(fields, field_y, field_x)
    accs = force_call("x", field_x, from_x, accs, kept_x, fields)
    acceleration, heating = force_call("z", field_z, from_z, accs, kept_z, fields)
    return (jnp.swapaxes(acceleration, 2, 3), heating)


def solution(mesh):
    in_specs = (
        P("gx", "gy", "gz", None, None),
        P("gx", "gy", "gz", None, None),
        P("gx", "gy", "gz", None),
        P("gx", "gy", "gz", None),
        P("gx", "gy", "gz", None),
        P("gx", "gy", "gz", None),
        P("gx", "gy", "gz", None),
        P("gx", "gy", "gz"),
    )
    out_specs = (P("gx", "gy", "gz", None, None), P("gx", "gy", "gz", None))
    return jax.shard_map(
        per_device, mesh=mesh, in_specs=in_specs, out_specs=out_specs, check_vma=False
    )
```

```python
import functools
import math

import jax
import jax.numpy as jnp
from jax import lax
from jax.experimental import pallas as pl
from jax.experimental.pallas import tpu as pltpu
from jax.sharding import PartitionSpec as P

kernel_norm = 21.0 / (16.0 * math.pi)
pressure_factor = 2.0 / 3.0
ridge_factor = 0.1
pair_scale = -160.0 * kernel_norm

LIMIT = 16 * 1024 * 1024
PACK_LIMIT = 63 * 1024 * 1024 - 65536
AXES = ("gx", "gy", "gz")
X, Y, Z, H, V, M, FLAGS = range(7)
PR, CA, CX, CY, CZ, VX, VY, VZ = range(8)


def code_of(step):
    index = (step[0] + 1) * 9 + (step[1] + 1) * 3 + step[2] + 1
    return index if index < 13 else index - 1


def swap(array, axis, phase):
    count = lax.axis_size(axis)
    pairs = []
    for first in range(phase, count, 2):
        second = (first + 1) % count
        pairs += [(first, second), (second, first)]
    return lax.ppermute(array, axis, pairs)


def swaps(array, axis):
    count = lax.axis_size(axis)
    if count == 2:
        return [swap(array, axis, 0)]
    return [swap(array, axis, 1), swap(array, axis, 0)][::-1]


def beside(get, step, axis):
    if step == 0:
        return get(0)
    if lax.axis_size(axis) == 2:
        return get(1)
    even = lax.axis_index(axis) % 2 == 0
    first, second = (1, 2) if step == 1 else (2, 1)
    return jnp.where(even, get(first), get(second))


def split(values, parts):
    pieces = []
    for _ in range(parts - 1):
        piece = values.astype(jnp.bfloat16).astype(jnp.float32)
        pieces.append(piece)
        values = values - piece
    return pieces + [values]


def stacked(parts):
    return jnp.concatenate(parts, axis=0).astype(jnp.bfloat16)


def left_form(features):
    high, middle, low = split(features, 3)
    return stacked([high, high, middle, high, low, middle]).T


def right_form(features):
    high, middle, low = split(features, 3)
    return stacked([high, middle, high, low, high, middle])


def pair_matrix(features):
    return jnp.concatenate(split(features, 2), axis=0).astype(jnp.bfloat16)


def feature_rows(features):
    rows = stacked(split(features, 3))
    return jnp.concatenate([rows, rows], axis=1)


def dot(left, right):
    return jnp.dot(left, right, preferred_element_type=jnp.float32)


def rows_of(tile, first, count=1):
    return [tile[k : k + 1] for k in range(first, first + count)]


def block_list(stage, leaves):
    blocks = []
    for dx in (-1, 0, 1):
        for dy in (-1, 0, 1):
            for leaf in range(leaves):
                for dz in (-1, 0, 1):
                    level = leaf + dz
                    if level < 0 or level >= leaves:
                        kind = "z"
                    elif dx:
                        kind = "x"
                    elif dy:
                        kind = "y"
                    else:
                        kind = "own"
                    if kind == stage:
                        blocks.append((leaf, (dx, dy, dz)))
    return blocks


def tile_at(refs, stage, dx, dy, level, leaves):
    def along_x(kx):
        def along_y(ky):
            if stage == "own":
                return refs[0][level]
            if stage == "y":
                return refs[ky - 1][level]
            if stage == "x":
                return refs[kx - 1][ky, level]
            ny = 1 if lax.axis_size("gy") == 2 else 2
            column = kx * (1 + ny) + ky
            even = lax.axis_index("gz") % 2 == 0
            above = level >= leaves
            return jnp.where(
                even, refs[0 if above else 1][column], refs[1 if above else 0][column]
            )

        return beside(along_y, dy, "gy")

    return beside(along_x, dx, "gx")


def tile_key(dx, dy, level):
    if lax.axis_size("gx") == 2:
        dx = abs(dx)
    if lax.axis_size("gy") == 2:
        dy = abs(dy)
    return (dx, dy, level)


def plan(stage, leaves):
    groups = {}
    for number, (leaf, step) in enumerate(block_list(stage, leaves)):
        key = tile_key(step[0], step[1], leaf + step[2])
        groups.setdefault(key, []).append((number, leaf, step))
    return list(groups.items())


def level_centre(level, leaves):
    return float(level) - 0.5 * (leaves - 1)


def pair_weight(own_tile, tile, step):
    if step == (0, 0, 0):
        return None
    code = code_of(step)
    weight = own_tile[FLAGS : FLAGS + 1, code : code + 1] + tile[FLAGS : FLAGS + 1, 25 - code : 26 - code]
    return jnp.broadcast_to(weight, (48, tile.shape[1]))


def add_weighted(acc, leaf, sums, weight):
    acc[leaf] = acc[leaf] + (sums if weight is None else sums * weight)


def place_rows(tile, dx, dy, level, leaves):
    centre = (float(dx), float(dy), level_centre(level, leaves))
    return [row + (part - 0.5) for row, part in zip(rows_of(tile, X, 3), centre)]


def moment_features(tile, dx, dy, level, leaves):
    x, y, z = place_rows(tile, dx, dy, level, leaves)
    (v, m) = rows_of(tile, V, 2)
    vx, vy, vz = v * x, v * y, v * z
    rows = [v, vx, vy, vz, vx * x, vx * y, vx * z, vy * y, vy * z, vz * z, m]
    return feature_rows(jnp.concatenate(rows + [jnp.zeros_like(v)] * 5, axis=0))


def moment_body(stage, leaves, per_leaf, own, sources, acc, w_out, g_out):
    one = jnp.ones((1, per_leaf), jnp.float32)
    zero = jnp.zeros((1, per_leaf), jnp.float32)
    number = 0
    widths = {}
    for leaf in range(leaves):
        smooth = rows_of(own[leaf], H)[0]
        widths[leaf] = right_form(
            jnp.concatenate([zero, smooth, zero, zero, zero, one, zero, zero], axis=0)
        )
    for (dx, dy, level), blocks in plan(stage, leaves):
        tile = tile_at(sources, stage, dx, dy, level, leaves)
        xj, yj, zj = [row - 0.5 for row in rows_of(tile, X, 3)]
        near = xj * xj + yj * yj + zj * zj
        left = left_form(
            jnp.concatenate([near, one, xj, yj, zj, tile[H : H + 1], zero, zero], axis=0)
        )
        inverses = {}
        features = {}
        for number, leaf, step in blocks:
            if leaf not in inverses:
                inverses[leaf] = 1.0 / dot(left, widths[leaf])
            if step[:2] not in features:
                features[step[:2]] = moment_features(tile, step[0], step[1], level, leaves)
            xi, yi, zi = [
                row - (0.5 + shift) for row, shift in zip(rows_of(own[leaf], X, 3), step)
            ]
            far = xi * xi + yi * yi + zi * zi
            right = right_form(
                jnp.concatenate(
                    [one, far, -2.0 * xi, -2.0 * yi, -2.0 * zi, zero, zero, zero], axis=0
                )
            )
            inverse = inverses[leaf]
            inverse_sq = inverse * inverse
            dist_sq = jnp.maximum(dot(left, right), 1e-30)
            dist = dist_sq * lax.rsqrt(dist_sq)
            remain = jnp.maximum(1.0 - dist * inverse, 0.0)
            edge = (inverse_sq * inverse) * (remain * remain * remain)
            pair_w = pair_matrix(edge * (remain * (0.2 * remain - 0.25)))
            w_out[number] = pair_w
            g_out[number] = edge * inverse_sq
            weight = pair_weight(own[leaf], tile, step)
            add_weighted(acc, leaf, dot(features[step[:2]], pair_w), weight)


def moment_kernel(stage, leaves, per_leaf, count, *refs):
    own = refs[0]
    sources = refs[1 : 1 + count] if count else (own,)
    rest = refs[1 + count :]
    if stage == "own":
        acc, w_out, g_out = rest
        acc[...] = jnp.zeros_like(acc)
    else:
        acc_in, acc, w_out, g_out = rest
        acc[...] = acc_in[...]
    moment_body(stage, leaves, per_leaf, own, sources, acc, w_out, g_out)


def corrections(moments, smooth, energy):
    density, zeroth, first_x, first_y, first_z, s_xx, s_xy, s_xz, s_yy, s_yz, s_zz = moments
    ridge_term = ridge_factor * smooth * smooth * zeroth
    s_xx = s_xx + ridge_term
    s_yy = s_yy + ridge_term
    s_zz = s_zz + ridge_term
    c_xx = s_yy * s_zz - s_yz * s_yz
    c_xy = s_yz * s_xz - s_xy * s_zz
    c_xz = s_xy * s_yz - s_yy * s_xz
    c_yy = s_xx * s_zz - s_xz * s_xz
    c_yz = s_xy * s_xz - s_xx * s_yz
    c_zz = s_xx * s_yy - s_xy * s_xy
    determinant = s_xx * c_xx + s_xy * c_xy + s_xz * c_xz
    solve_x = (c_xx * first_x + c_xy * first_y + c_xz * first_z) / determinant
    solve_y = (c_xy * first_x + c_yy * first_y + c_yz * first_z) / determinant
    solve_z = (c_xz * first_x + c_yz * first_y + c_zz * first_z) / determinant
    coef_a = 1.0 / (zeroth - (first_x * solve_x + first_y * solve_y + first_z * solve_z))
    pressure = pressure_factor * density * energy
    return [pressure, coef_a, -coef_a * solve_x, -coef_a * solve_y, -coef_a * solve_z]

def gathered(acc, leaf):
    sums = acc[leaf]
    return sums[0:16] + (sums[16:32] + sums[32:48])


def field_kernel(leaves, per_leaf, count, *refs):
    own = refs[0]
    sources = refs[1 : 1 + count]
    acc_in, extra, fields_out, w_out, g_out, acc = refs[1 + count :]
    acc[...] = acc_in[...]
    moment_body("z", leaves, per_leaf, own, sources, acc, w_out, g_out)
    columns = []
    for leaf in range(leaves):
        sums = gathered(acc, leaf)
        zeroth, fx, fy, fz, sxx, sxy, sxz, syy, syz, szz, density = rows_of(sums, 0, 11)
        x, y, z = place_rows(own[leaf], 0, 0, leaf, leaves)
        mx, my, mz = x * zeroth - fx, y * zeroth - fy, z * zeroth - fz
        columns.append(
            [
                density,
                zeroth,
                mx,
                my,
                mz,
                x * mx - x * fx + sxx,
                x * my - y * fx + sxy,
                x * mz - z * fx + sxz,
                y * my - y * fy + syy,
                y * mz - z * fy + syz,
                z * mz - z * fz + szz,
                own[leaf][H : H + 1],
                extra[leaf][3:4],
            ]
        )
    rows = [jnp.concatenate(parts, axis=0) for parts in zip(*columns)]
    fields = corrections(rows[:11], rows[11], rows[12])
    for leaf in range(leaves):
        for k, value in enumerate(fields):
            fields_out[leaf, k : k + 1, :] = value[leaf : leaf + 1]
        fields_out[leaf, VX : VZ + 1, :] = extra[leaf][0:3]


def force_body(stage, leaves, per_leaf, own, fields, sources, places, accs, w_in, g_in):
    one = jnp.ones((1, per_leaf), jnp.float32)
    acc_w, acc_g = accs
    for (dx, dy, level), blocks in plan(stage, leaves):
        tile = tile_at(places, stage, dx, dy, level, leaves)
        field = tile_at(sources, stage, dx, dy, level, leaves)
        xj, yj, zj = [row - 0.5 for row in rows_of(tile, X, 3)]
        pressure, coef, cx, cy, cz, vx, vy, vz = rows_of(field, 0, 8)
        volume = tile[V : V + 1]
        left = left_form(
            jnp.concatenate(
                [one, coef + (cx * xj + cy * yj + cz * zj), xj, yj, zj, cx, cy, cz], axis=0
            )
        )

        def weighted(a, b, c):
            first = volume * jnp.concatenate(
                [one, a, b, c, vx, vy, vz, a * vx + b * vy + c * vz], axis=0
            )
            return feature_rows(jnp.concatenate([first, pressure * first], axis=0))

        with_w = weighted(cx, cy, cz)
        with_g = {}
        for number, leaf, step in blocks:
            if step[:2] not in with_g:
                with_g[step[:2]] = weighted(*place_rows(tile, step[0], step[1], level, leaves))
            xi, yi, zi = [
                row - (0.5 + shift) for row, shift in zip(rows_of(own[leaf], X, 3), step)
            ]
            _, coef_i, cxi, cyi, czi = rows_of(fields[leaf], 0, 5)
            right = right_form(
                jnp.concatenate(
                    [coef_i + (cxi * xi + cyi * yi + czi * zi), one]
                    + [-cxi, -cyi, -czi, -xi, -yi, -zi],
                    axis=0,
                )
            )
            radial = pair_matrix(g_in[number] * dot(left, right))
            weight = pair_weight(own[leaf], tile, step)
            add_weighted(acc_w, leaf, dot(with_w, w_in[number]), weight)
            add_weighted(acc_g, leaf, dot(with_g[step[:2]], radial), weight)


def force_setup(stage, count, refs):
    own, fields = refs[0], refs[1]
    sources = refs[2 : 2 + count] if count else (fields,)
    places = refs[2 + count : 2 + 2 * count] if count else (own,)
    return own, fields, sources, places, refs[2 + 2 * count :]


def force_kernel(stage, leaves, per_leaf, count, *refs):
    own, fields, sources, places, rest = force_setup(stage, count, refs)
    if stage == "own":
        w_in, g_in, acc_w, acc_g = rest
        acc_w[...] = jnp.zeros_like(acc_w)
        acc_g[...] = jnp.zeros_like(acc_g)
    else:
        w_before, g_before, w_in, g_in, acc_w, acc_g = rest
        acc_w[...] = w_before[...]
        acc_g[...] = g_before[...]
    force_body(
        stage, leaves, per_leaf, own, fields, sources, places, (acc_w, acc_g), w_in, g_in
    )


def finish_kernel(leaves, per_leaf, count, *refs):
    own, fields, sources, places, rest = force_setup("z", count, refs)
    w_before, g_before, w_in, g_in, acceleration, heating, acc_w, acc_g = rest
    acc_w[...] = w_before[...]
    acc_g[...] = g_before[...]
    force_body(
        "z", leaves, per_leaf, own, fields, sources, places, (acc_w, acc_g), w_in, g_in
    )
    for leaf in range(leaves):
        tile = own[leaf]
        pressure, _, cx, cy, cz, vx, vy, vz = rows_of(fields[leaf], 0, 8)
        sums_w, sums_g = gathered(acc_w, leaf), gathered(acc_g, leaf)
        both_w = pressure * sums_w[0:8] + sums_w[8:16]
        both_g = pressure * sums_g[0:8] + sums_g[8:16]
        w_rows, g_rows = rows_of(both_w, 0, 8), rows_of(both_g, 0, 8)
        coefs = (cx, cy, cz)
        spots = place_rows(tile, 0, 0, leaf, leaves)
        ratio = tile[V : V + 1] / tile[M : M + 1]
        work = w_rows[7] + g_rows[7]
        for k, (coef, spot, speed) in enumerate(zip(coefs, spots, (vx, vy, vz))):
            force = (coef * w_rows[0] - w_rows[1 + k]) + (spot * g_rows[0] - g_rows[1 + k])
            work = work + speed * force - coef * w_rows[4 + k] - spot * g_rows[4 + k]
            acceleration[0, 0, k, leaf : leaf + 1, :] = (-0.5 * ratio) * force
        heating[0, 0, leaf : leaf + 1, :] = (0.25 * ratio) * work


def pack_kernel(leaves, per_leaf, *refs):
    inputs, out, extra, held, sems = refs[:8], refs[8], refs[9], refs[10:18], refs[18]
    neighbours, counts = held[6:8]
    copies = [
        pltpu.make_async_copy(source, target, sems.at[k])
        for k, (source, target) in enumerate(zip(inputs, held))
    ]
    for copy in copies[::-1]:
        copy.start()
    for copy in copies[6:]:
        copy.wait()
    lane = lax.broadcasted_iota(jnp.int32, (1, per_leaf), 1)
    for leaf in range(leaves):
        flags = jnp.zeros((1, per_leaf), jnp.float32)
        for slot in range(neighbours.shape[3]):
            code = jnp.where(slot < counts[0, 0, leaf], neighbours[0, 0, leaf, slot], -1)
            flags = flags + jnp.where(lane == code, 1.0, 0.0)
        out[leaf, FLAGS : FLAGS + 1, :] = flags
        out[leaf, FLAGS + 1 : FLAGS + 2, :] = jnp.zeros((1, per_leaf), jnp.float32)
        extra[leaf, 4:8, :] = jnp.zeros((4, per_leaf), jnp.float32)
    for copy in copies[:6]:
        copy.wait()
    offsets, velocity, masses, volumes, energies, smoothing = held[:6]
    for leaf in range(leaves):
        one = slice(leaf, leaf + 1)
        for part in range(3):
            out[leaf, part : part + 1, :] = offsets[0, 0, part, one]
            extra[leaf, part : part + 1, :] = velocity[0, 0, part, one]
        out[leaf, H : H + 1, :] = smoothing[0, 0, one]
        out[leaf, V : V + 1, :] = pair_scale * volumes[0, 0, one]
        out[leaf, M : M + 1, :] = pair_scale * masses[0, 0, one]
        extra[leaf, 3:4, :] = energies[0, 0, one]


def per_device(offsets, velocity, masses, volumes, energies, smoothing, neighbours, counts):
    leaves, per_leaf = masses.shape[2], masses.shape[3]
    f32, bf16 = jnp.float32, jnp.bfloat16
    vmem = pl.BlockSpec(memory_space=pltpu.VMEM)
    hbm = pl.BlockSpec(memory_space=pltpu.HBM)
    params = pltpu.CompilerParams(vmem_limit_bytes=LIMIT)
    parity = lax.axis_index("gz") % 2 == 0
    offsets = jnp.swapaxes(offsets, 2, 3)
    velocity = jnp.swapaxes(velocity, 2, 3)

    def cost(blocks, ops):
        return pl.CostEstimate(
            flops=blocks * per_leaf * per_leaf * ops, bytes_accessed=blocks * 4096, transcendentals=0
        )

    inputs = (offsets, velocity, masses, volumes, energies, smoothing)
    own, extra = pl.pallas_call(
        functools.partial(pack_kernel, leaves, per_leaf),
        out_shape=[pltpu.VMEM((leaves, 8, per_leaf), f32)] * 2,
        in_specs=[hbm] * 8,
        out_specs=[vmem] * 2,
        scratch_shapes=[pltpu.VMEM(array.shape, f32) for array in inputs]
        + [pltpu.SMEM(array.shape, jnp.int32) for array in (neighbours, counts)]
        + [pltpu.SemaphoreType.DMA((8,))],
        compiler_params=pltpu.CompilerParams(vmem_limit_bytes=PACK_LIMIT),
        name="pack",
    )(*inputs, neighbours, counts)

    def exchange_y(tile):
        return swaps(tile, "gy")

    def exchange_x(tile, from_y):
        return swaps(jnp.stack([tile] + from_y, axis=0), "gx")

    def exchange_z(tile, from_y, from_x):
        column = jnp.concatenate([jnp.stack([tile] + from_y, axis=0)] + from_x, axis=0)
        bottom, top = column[:, 0], column[:, leaves - 1]
        far = swap(jnp.where(parity, bottom, top), "gz", 1)
        near = swap(jnp.where(parity, top, bottom), "gz", 0)
        return [near, far]

    stages = ("own", "y", "x", "z")
    sizes = {stage: len(block_list(stage, leaves)) for stage in stages}
    acc_shape = jax.ShapeDtypeStruct((leaves, 48, per_leaf), f32)
    acc_scratch = pltpu.VMEM((leaves, 48, per_leaf), f32)

    def moment_call(stage, sources, acc):
        size = sizes[stage]
        kept = [
            jax.ShapeDtypeStruct((size, 2 * per_leaf, per_leaf), bf16),
            jax.ShapeDtypeStruct((size, per_leaf, per_leaf), f32),
        ]
        operands = [own] + list(sources) + ([] if acc is None else [acc])
        scratch = []
        if stage == "z":
            body = functools.partial(field_kernel, leaves, per_leaf, len(sources))
            operands += [extra]
            first = jax.ShapeDtypeStruct((leaves, 8, per_leaf), f32)
            scratch = [acc_scratch]
        else:
            body = functools.partial(moment_kernel, stage, leaves, per_leaf, len(sources))
            first = acc_shape
        return pl.pallas_call(
            body,
            out_shape=[first] + kept,
            in_specs=[vmem] * len(operands),
            out_specs=[vmem] * 3,
            scratch_shapes=scratch,
            compiler_params=params,
            cost_estimate=cost(size, 55),
            name="moments_" + stage,
        )(*operands)

    def force_call(stage, sources, places, accs, kept, fields):
        size = sizes[stage]
        operands = [own, fields] + list(sources) + list(places) + list(accs) + list(kept)
        scratch = []
        if stage == "z":
            body = functools.partial(finish_kernel, leaves, per_leaf, len(sources))
            out = [
                jax.ShapeDtypeStruct((1, 1, 3, leaves, per_leaf), f32),
                jax.ShapeDtypeStruct((1, 1, leaves, per_leaf), f32),
            ]
            scratch = [acc_scratch] * 2
        else:
            body = functools.partial(force_kernel, stage, leaves, per_leaf, len(sources))
            out = [acc_shape] * 2
        return pl.pallas_call(
            body,
            out_shape=out,
            in_specs=[vmem] * len(operands),
            out_specs=[vmem] * len(out),
            scratch_shapes=scratch,
            compiler_params=params,
            cost_estimate=cost(size, 36),
            name="force_" + stage,
        )(*operands)

    from_y = exchange_y(own)
    acc, *kept_own = moment_call("own", [], None)
    from_y, acc = lax.optimization_barrier((from_y, acc))
    from_x = exchange_x(own, from_y)
    acc, *kept_y = moment_call("y", from_y, acc)
    from_x, acc = lax.optimization_barrier((from_x, acc))
    from_z = exchange_z(own, from_y, from_x)
    acc, *kept_x = moment_call("x", from_x, acc)
    fields, *kept_z = moment_call("z", from_z, acc)

    field_y = exchange_y(fields)
    accs = force_call("own", [], [], [], kept_own, fields)
    field_y, accs = lax.optimization_barrier((field_y, accs))
    field_x = exchange_x(fields, field_y)
    accs = force_call("y", field_y, from_y, accs, kept_y, fields)
    field_x, accs = lax.optimization_barrier((field_x, accs))
    field_z = exchange_z(fields, field_y, field_x)
    accs = force_call("x", field_x, from_x, accs, kept_x, fields)
    acceleration, heating = force_call("z", field_z, from_z, accs, kept_z, fields)
    return (jnp.swapaxes(acceleration, 2, 3), heating)


def solution(mesh):
    in_specs = (
        P("gx", "gy", "gz", None, None),
        P("gx", "gy", "gz", None, None),
        P("gx", "gy", "gz", None),
        P("gx", "gy", "gz", None),
        P("gx", "gy", "gz", None),
        P("gx", "gy", "gz", None),
        P("gx", "gy", "gz", None),
        P("gx", "gy", "gz"),
    )
    out_specs = (P("gx", "gy", "gz", None, None), P("gx", "gy", "gz", None))
    return jax.shard_map(
        per_device, mesh=mesh, in_specs=in_specs, out_specs=out_specs, check_vma=False
    )
```

```python
import functools
import math

import jax
import jax.numpy as jnp
from jax import lax
from jax.experimental import pallas as pl
from jax.experimental.pallas import tpu as pltpu
from jax.sharding import PartitionSpec as P

kernel_norm = 21.0 / (16.0 * math.pi)
pressure_factor = 2.0 / 3.0
ridge_factor = 0.1
pair_scale = -160.0 * kernel_norm

LIMIT = 16 * 1024 * 1024
PACK_LIMIT = 63 * 1024 * 1024 - 65536
AXES = ("gx", "gy", "gz")
X, Y, Z, H, V, M, FLAGS = range(7)
VX, VY, VZ, PR, CA, CX, CY, CZ = range(8)


def code_of(step):
    index = (step[0] + 1) * 9 + (step[1] + 1) * 3 + step[2] + 1
    return index if index < 13 else index - 1


def swap(array, axis, phase):
    count = lax.axis_size(axis)
    pairs = []
    for first in range(phase, count, 2):
        second = (first + 1) % count
        pairs += [(first, second), (second, first)]
    return lax.ppermute(array, axis, pairs)


def swaps(array, axis):
    count = lax.axis_size(axis)
    if count == 2:
        return [swap(array, axis, 0)]
    return [swap(array, axis, 1), swap(array, axis, 0)][::-1]


def beside(get, step, axis):
    if step == 0:
        return get(0)
    if lax.axis_size(axis) == 2:
        return get(1)
    even = lax.axis_index(axis) % 2 == 0
    first, second = (1, 2) if step == 1 else (2, 1)
    return jnp.where(even, get(first), get(second))


def split(values, parts):
    pieces = []
    for _ in range(parts - 1):
        piece = values.astype(jnp.bfloat16).astype(jnp.float32)
        pieces.append(piece)
        values = values - piece
    return pieces + [values]


def stacked(parts):
    return jnp.concatenate(parts, axis=0).astype(jnp.bfloat16)


def left_form(features):
    high, middle, low = split(features, 3)
    return stacked([high, high, middle, high, low, middle]).T


def right_form(features):
    high, middle, low = split(features, 3)
    return stacked([high, middle, high, low, high, middle])


def pair_matrix(values):
    return jnp.concatenate(split(values, 2), axis=0).astype(jnp.bfloat16)


def feature_rows(first, second):
    pieces = [piece for pair in zip(split(first, 3), split(second, 3)) for piece in pair]
    rows = stacked(pieces)
    return jnp.concatenate([rows, rows], axis=1)


def dot(left, right):
    return jnp.dot(left, right, preferred_element_type=jnp.float32)


def row_index(per_leaf):
    return lax.broadcasted_iota(jnp.int32, (8, per_leaf), 0)


def chosen(pairs, other):
    for condition, value in pairs[::-1]:
        other = jnp.where(condition, value, other)
    return other


def front_sum(tile, row):
    return jnp.sum(jnp.where(row < 3, tile, 0.0), axis=0, keepdims=True)


def at_front(row, values):
    x, y, z = values
    return chosen([(row == 0, x), (row == 1, y), (row == 2, z)], 0.0)


def rows_of(tile, first, count=1):
    return [tile[k : k + 1] for k in range(first, first + count)]


STAGES = ("own", "y", "x", "z")


def columns_of(stage):
    return {"own": (0,), "y": (0,), "x": (-1, 1), "z": (-1, 0, 1)}[stage]


def slots_of(stage, leaves):
    slots = {}
    for dy in (-1, 0, 1):
        for leaf in range(leaves):
            for level in range(leaf - 1, leaf + 2):
                outside = level < 0 or level >= leaves
                if outside != (stage == "z"):
                    continue
                if (stage == "own" and dy) or (stage == "y" and not dy):
                    continue
                key = (abs(dy) if lax.axis_size("gy") == 2 else dy, level)
                slots.setdefault(key, []).append((leaf, dy))
    return list(slots.items())


def slot_blocks(stage, leaves):
    slots = slots_of(stage, leaves)
    return [(k, level, leaf, dy) for k, ((_, level), blocks) in enumerate(slots) for leaf, dy in blocks]


def tile_at(refs, stage, dx, dy, level, leaves):
    def along_x(kx):
        def along_y(ky):
            if stage == "own":
                return refs[0][level]
            if stage == "y":
                return refs[ky - 1][level]
            if stage == "x":
                return refs[kx - 1][ky, level]
            ny = 1 if lax.axis_size("gy") == 2 else 2
            column = kx * (1 + ny) + ky
            even = lax.axis_index("gz") % 2 == 0
            above = level >= leaves
            return jnp.where(
                even, refs[0 if above else 1][column], refs[1 if above else 0][column]
            )

        return beside(along_y, dy, "gy")

    return beside(along_x, dx, "gx")


def place_shift(dx, dy, level, leaves):
    return (dx, float(dy), float(level) - 0.5 * (leaves - 1))


def centred(tile, row):
    return tile - jnp.where(row < 3, 0.5, 0.0)


def gather_tiles(tiles, sources, stage, leaves):
    slots = slots_of(stage, leaves)
    for column, dx in enumerate(columns_of(stage)):
        for k, ((dy, level), _) in enumerate(slots):
            tiles[column * len(slots) + k] = tile_at(sources, stage, dx, dy, level, leaves)


def find_weights(weights, own, tiles, stage, leaves):
    slots = slots_of(stage, leaves)
    blocks = slot_blocks(stage, leaves)
    for column, dx in enumerate(columns_of(stage)):
        for b, (k, level, leaf, dy) in enumerate(blocks):
            step = (dx, dy, level - leaf)
            if step == (0, 0, 0):
                weight = jnp.ones((1, 1), jnp.float32)
            else:
                code = code_of(step)
                tile = tiles[column * len(slots) + k]
                weight = (
                    own[leaf][FLAGS : FLAGS + 1, code : code + 1]
                    + tile[FLAGS : FLAGS + 1, 25 - code : 26 - code]
                )
            weights[column * len(blocks) + b] = jnp.broadcast_to(weight, weights.shape[1:])


def add_weighted(acc, leaf, sums, weight):
    for k in range(6):
        part = slice(8 * k, 8 * k + 8)
        acc[leaf, part, :] = acc[leaf, part, :] + sums[part] * weight


def over_columns(stage, step_fn):
    columns = columns_of(stage)
    if len(columns) == 1:
        step_fn(0, float(columns[0]))
        return
    pace = columns[1] - columns[0]

    def body(column, carry):
        step_fn(column, (column * pace + columns[0]).astype(jnp.float32))
        return carry

    lax.fori_loop(0, len(columns), body, 0)


def moment_rights(own, leaves, row, rights):
    for stage, right in zip(STAGES, rights):
        blocks = slot_blocks(stage, leaves)
        for column, dx in enumerate(columns_of(stage)):
            for b, (_, level, leaf, dy) in enumerate(blocks):
                shift = at_front(row, (0.5 + dx, 0.5 + dy, 0.5 + level - leaf))
                spot = own[leaf] - shift
                far = front_sum(spot * spot, row)
                right[column * len(blocks) + b] = right_form(
                    chosen([(row < 3, -2.0 * spot), (row == 4, 1.0), (row == 5, far)], 0.0)
                )


def moment_body(stage, leaves, per_leaf, own, sources, right, acc, w_out, g_out, tiles, weights):
    row = row_index(per_leaf)
    gather_tiles(tiles, sources, stage, leaves)
    find_weights(weights, own, tiles, stage, leaves)
    widths = [
        right_form(chosen([(row == 3, 1.0), (row == 5, own[leaf][H : H + 1])], 0.0))
        for leaf in range(leaves)
    ]
    slots = slots_of(stage, leaves)
    count = len(slot_blocks(stage, leaves))

    def step_fn(column, dx):
        number = column * count
        for k, ((_, level), blocks) in enumerate(slots):
            tile = tiles[column * len(slots) + k]
            spot = centred(tile, row)
            near = front_sum(spot * spot, row)
            left = left_form(chosen([(row < 4, spot), (row == 4, near), (row == 5, 1.0)], 0.0))
            volume, mass = tile[V : V + 1], tile[M : M + 1]
            inverses, features = {}, {}
            for leaf, dy in blocks:
                if leaf not in inverses:
                    inverses[leaf] = 1.0 / dot(left, widths[leaf])
                if dy not in features:
                    x, y, z = [
                        part + shift
                        for part, shift in zip(
                            rows_of(spot, X, 3), place_shift(dx, dy, level, leaves)
                        )
                    ]
                    first = chosen(
                        [(row == 0, 1.0), ((row == 2) | (row == 7), y), (row == 3, z)], x
                    ) * chosen(
                        [(row < 4, 1.0), (row == 4, x), (row == 6, z)], y
                    )
                    second = chosen([(row == 0, y), (row == 1, z)], 1.0) * jnp.where(
                        row < 2, z, 1.0
                    )
                    features[dy] = feature_rows(
                        first * volume,
                        second * chosen([(row < 2, volume), (row == 2, mass)], 0.0),
                    )
                inverse = inverses[leaf]
                inverse_sq = inverse * inverse
                dist_sq = jnp.maximum(dot(left, right[number]), 1e-30)
                dist = dist_sq * lax.rsqrt(dist_sq)
                remain = jnp.maximum(1.0 - dist * inverse, 0.0)
                edge = (inverse_sq * inverse) * (remain * remain * remain)
                pair_w = pair_matrix(edge * (remain * (remain - 1.25)))
                w_out[number] = pair_w
                g_out[number] = edge * inverse_sq
                add_weighted(acc, leaf, dot(features[dy], pair_w), weights[number])
                number = number + 1

    over_columns(stage, step_fn)


def moment_own_kernel(leaves, per_leaf, own, acc, w_out, g_out, *refs):
    rights, (tiles, weights) = refs[:4], refs[4:]
    acc[...] = jnp.zeros_like(acc)
    moment_rights(own, leaves, row_index(per_leaf), rights)
    moment_body(
        "own", leaves, per_leaf, own, (own,), rights[0], acc, w_out, g_out, tiles, weights
    )


def moment_kernel(stage, leaves, per_leaf, count, *refs):
    own, sources = refs[0], refs[1 : 1 + count]
    right, acc_in, acc, w_out, g_out, tiles, weights = refs[1 + count :]
    acc[...] = acc_in[...]
    moment_body(
        stage, leaves, per_leaf, own, sources, right, acc, w_out, g_out, tiles, weights
    )


def corrections(moments, smooth, energy):
    density, zeroth, first_x, first_y, first_z, s_xx, s_xy, s_xz, s_yy, s_yz, s_zz = moments
    ridge_term = ridge_factor * smooth * smooth * zeroth
    s_xx = s_xx + ridge_term
    s_yy = s_yy + ridge_term
    s_zz = s_zz + ridge_term
    c_xx = s_yy * s_zz - s_yz * s_yz
    c_xy = s_yz * s_xz - s_xy * s_zz
    c_xz = s_xy * s_yz - s_yy * s_xz
    c_yy = s_xx * s_zz - s_xz * s_xz
    c_yz = s_xy * s_xz - s_xx * s_yz
    c_zz = s_xx * s_yy - s_xy * s_xy
    determinant = s_xx * c_xx + s_xy * c_xy + s_xz * c_xz
    solve_x = (c_xx * first_x + c_xy * first_y + c_xz * first_z) / determinant
    solve_y = (c_xy * first_x + c_yy * first_y + c_yz * first_z) / determinant
    solve_z = (c_xz * first_x + c_yz * first_y + c_zz * first_z) / determinant
    coef_a = 1.0 / (zeroth - (first_x * solve_x + first_y * solve_y + first_z * solve_z))
    pressure = pressure_factor * density * energy
    return [pressure, coef_a, -coef_a * solve_x, -coef_a * solve_y, -coef_a * solve_z]

def gathered(acc, leaf):
    sums = acc[leaf]
    return sums[0:16] + (sums[16:32] + sums[32:48])


def own_place(tile, leaf, leaves):
    shift = place_shift(0.0, 0, leaf, leaves)
    return [part + (move - 0.5) for part, move in zip(rows_of(tile, X, 3), shift)]


def field_kernel(leaves, per_leaf, count, *refs):
    own, sources = refs[0], refs[1 : 1 + count]
    right, acc_in, extra, fields_out, w_out, g_out, tiles, weights, acc = refs[1 + count :]
    acc[...] = acc_in[...]
    moment_body("z", leaves, per_leaf, own, sources, right, acc, w_out, g_out, tiles, weights)
    columns = []
    for leaf in range(leaves):
        sums = gathered(acc, leaf)
        zeroth, fx, fy, fz, sxx, sxy, sxz, syy, syz, szz, density = rows_of(sums, 0, 11)
        x, y, z = own_place(own[leaf], leaf, leaves)
        mx, my, mz = x * zeroth - fx, y * zeroth - fy, z * zeroth - fz
        columns.append(
            [
                density,
                zeroth,
                mx,
                my,
                mz,
                x * mx - x * fx + sxx,
                x * my - y * fx + sxy,
                x * mz - z * fx + sxz,
                y * my - y * fy + syy,
                y * mz - z * fy + syz,
                z * mz - z * fz + szz,
                own[leaf][H : H + 1],
                extra[leaf][3:4],
            ]
        )
    rows = [jnp.concatenate(parts, axis=0) for parts in zip(*columns)]
    fields = corrections([0.2 * part for part in rows[:11]], rows[11], rows[12])
    for leaf in range(leaves):
        fields_out[leaf, VX : VZ + 1, :] = extra[leaf][0:3]
        for k, value in enumerate(fields):
            fields_out[leaf, PR + k : PR + k + 1, :] = value[leaf : leaf + 1]


def force_rights(own, fields, leaves, row, rights):
    for stage, right in zip(STAGES, rights):
        blocks = slot_blocks(stage, leaves)
        for column, dx in enumerate(columns_of(stage)):
            for b, (_, level, leaf, dy) in enumerate(blocks):
                shift = at_front(row, (0.5 + dx, 0.5 + dy, 0.5 + level - leaf))
                spot = own[leaf] - shift
                coefs = pltpu.roll(fields[leaf], 3, 0)
                full = fields[leaf][CA : CA + 1] + front_sum(coefs * spot, row)
                right[column * len(blocks) + b] = right_form(
                    chosen(
                        [(row < 3, -coefs), (row == 3, full), (row == 4, 1.0)],
                        -pltpu.roll(spot, 5, 0),
                    )
                )


def force_body(stage, leaves, per_leaf, own, sources, places, right, accs, w_in, g_in, scratch):
    row = row_index(per_leaf)
    tiles, field_tiles, weights = scratch
    acc_w, acc_g = accs
    gather_tiles(tiles, places, stage, leaves)
    gather_tiles(field_tiles, sources, stage, leaves)
    find_weights(weights, own, tiles, stage, leaves)
    slots = slots_of(stage, leaves)
    count = len(slot_blocks(stage, leaves))

    def step_fn(column, dx):
        number = column * count
        for k, ((_, level), blocks) in enumerate(slots):
            tile = tiles[column * len(slots) + k]
            field = field_tiles[column * len(slots) + k]
            spot = centred(tile, row)
            coefs = pltpu.roll(field, 3, 0)
            volume, pressure = tile[V : V + 1], field[PR : PR + 1]
            full = field[CA : CA + 1] + front_sum(coefs * spot, row)
            left = left_form(
                chosen([(row < 3, spot), (row == 3, 1.0), (row == 4, full)], field)
            )

            def weighted(front, back, factor):
                first = (factor * volume) * chosen(
                    [
                        (row < 3, field),
                        (row == 3, 1.0),
                        (row == 4, front_sum(front * field, row)),
                    ],
                    back,
                )
                return feature_rows(first, pressure * first)

            with_w = weighted(coefs, field, 0.2)
            with_g = {}
            for leaf, dy in blocks:
                if dy not in with_g:
                    front = spot + at_front(row, place_shift(dx, dy, level, leaves))
                    with_g[dy] = weighted(front, pltpu.roll(front, 5, 0), 1.0)
                radial = pair_matrix(g_in[number] * dot(left, right[number]))
                weight = weights[number]
                add_weighted(acc_w, leaf, dot(with_w, w_in[number]), weight)
                add_weighted(acc_g, leaf, dot(with_g[dy], radial), weight)
                number = number + 1

    over_columns(stage, step_fn)


def force_own_kernel(leaves, per_leaf, own, fields, w_in, g_in, acc_w, acc_g, *refs):
    rights, scratch = refs[:4], refs[4:]
    acc_w[...] = jnp.zeros_like(acc_w)
    acc_g[...] = jnp.zeros_like(acc_g)
    force_rights(own, fields, leaves, row_index(per_leaf), rights)
    force_body(
        "own",
        leaves,
        per_leaf,
        own,
        (fields,),
        (own,),
        rights[0],
        (acc_w, acc_g),
        w_in,
        g_in,
        scratch,
    )


def force_kernel(stage, leaves, per_leaf, count, *refs):
    own, sources, places = refs[0], refs[1 : 1 + count], refs[1 + count : 1 + 2 * count]
    right, w_before, g_before, w_in, g_in, acc_w, acc_g, *scratch = refs[1 + 2 * count :]
    acc_w[...] = w_before[...]
    acc_g[...] = g_before[...]
    accs = (acc_w, acc_g)
    force_body(
        stage, leaves, per_leaf, own, sources, places, right, accs, w_in, g_in, scratch
    )


def finish_kernel(leaves, per_leaf, count, *refs):
    own, sources, places = refs[0], refs[1 : 1 + count], refs[1 + count : 1 + 2 * count]
    rest = refs[1 + 2 * count :]
    right, w_before, g_before, w_in, g_in, fields, acceleration, heating = rest[:8]
    scratch, accs = rest[8:11], rest[11:13]
    accs[0][...] = w_before[...]
    accs[1][...] = g_before[...]
    force_body("z", leaves, per_leaf, own, sources, places, right, accs, w_in, g_in, scratch)
    for leaf in range(leaves):
        tile = own[leaf]
        vx, vy, vz, pressure, _, cx, cy, cz = rows_of(fields[leaf], 0, 8)
        sums_w, sums_g = [gathered(acc, leaf) for acc in accs]
        w_rows = rows_of(pressure * sums_w[0:8] + sums_w[8:16], 0, 8)
        g_rows = rows_of(pressure * sums_g[0:8] + sums_g[8:16], 0, 8)
        spots = own_place(tile, leaf, leaves)
        ratio = tile[V : V + 1] / tile[M : M + 1]
        work = w_rows[4] + g_rows[4]
        for k, (coef, spot, speed) in enumerate(zip((cx, cy, cz), spots, (vx, vy, vz))):
            force = (coef * w_rows[3] - w_rows[5 + k]) + (spot * g_rows[3] - g_rows[5 + k])
            work = work + speed * force - coef * w_rows[k] - spot * g_rows[k]
            acceleration[0, 0, k, leaf : leaf + 1, :] = (-0.5 * ratio) * force
        heating[0, 0, leaf : leaf + 1, :] = (0.25 * ratio) * work


def pack_kernel(leaves, per_leaf, *refs):
    inputs, out, extra, held, sems = refs[:8], refs[8], refs[9], refs[10:18], refs[18]
    neighbours, counts = held[6:8]
    copies = [
        pltpu.make_async_copy(source, target, sems.at[k])
        for k, (source, target) in enumerate(zip(inputs, held))
    ]
    for copy in copies[::-1]:
        copy.start()
    for copy in copies[6:]:
        copy.wait()
    lane = lax.broadcasted_iota(jnp.int32, (1, per_leaf), 1)
    for leaf in range(leaves):
        flags = jnp.zeros((1, per_leaf), jnp.float32)
        for slot in range(neighbours.shape[3]):
            code = jnp.where(slot < counts[0, 0, leaf], neighbours[0, 0, leaf, slot], -1)
            flags = flags + jnp.where(lane == code, 1.0, 0.0)
        out[leaf, FLAGS : FLAGS + 1, :] = flags
        out[leaf, FLAGS + 1 : FLAGS + 2, :] = jnp.zeros((1, per_leaf), jnp.float32)
        extra[leaf, 4:8, :] = jnp.zeros((4, per_leaf), jnp.float32)
    for copy in copies[:6]:
        copy.wait()
    offsets, velocity, masses, volumes, energies, smoothing = held[:6]
    for leaf in range(leaves):
        one = slice(leaf, leaf + 1)
        for part in range(3):
            out[leaf, part : part + 1, :] = offsets[0, 0, part, one]
            extra[leaf, part : part + 1, :] = velocity[0, 0, part, one]
        out[leaf, H : H + 1, :] = smoothing[0, 0, one]
        out[leaf, V : V + 1, :] = pair_scale * volumes[0, 0, one]
        out[leaf, M : M + 1, :] = pair_scale * masses[0, 0, one]
        extra[leaf, 3:4, :] = energies[0, 0, one]


def per_device(offsets, velocity, masses, volumes, energies, smoothing, neighbours, counts):
    leaves, per_leaf = masses.shape[2], masses.shape[3]
    f32, bf16 = jnp.float32, jnp.bfloat16
    vmem = pl.BlockSpec(memory_space=pltpu.VMEM)
    hbm = pl.BlockSpec(memory_space=pltpu.HBM)
    params = pltpu.CompilerParams(vmem_limit_bytes=LIMIT)
    parity = lax.axis_index("gz") % 2 == 0
    offsets = jnp.swapaxes(offsets, 2, 3)
    velocity = jnp.swapaxes(velocity, 2, 3)

    def cost(blocks, ops):
        return pl.CostEstimate(
            flops=blocks * per_leaf * per_leaf * ops, bytes_accessed=blocks * 4096, transcendentals=0
        )

    inputs = (offsets, velocity, masses, volumes, energies, smoothing)
    own, extra = pl.pallas_call(
        functools.partial(pack_kernel, leaves, per_leaf),
        out_shape=[pltpu.VMEM((leaves, 8, per_leaf), f32)] * 2,
        in_specs=[hbm] * 8,
        out_specs=[vmem] * 2,
        scratch_shapes=[pltpu.VMEM(array.shape, f32) for array in inputs]
        + [pltpu.SMEM(array.shape, jnp.int32) for array in (neighbours, counts)]
        + [pltpu.SemaphoreType.DMA((8,))],
        compiler_params=pltpu.CompilerParams(vmem_limit_bytes=PACK_LIMIT),
        name="pack",
    )(*inputs, neighbours, counts)

    def exchange_y(tile):
        return swaps(tile, "gy")

    def exchange_x(tile, from_y):
        return swaps(jnp.stack([tile] + from_y, axis=0), "gx")

    def exchange_z(tile, from_y, from_x):
        column = jnp.concatenate([jnp.stack([tile] + from_y, axis=0)] + from_x, axis=0)
        bottom, top = column[:, 0], column[:, leaves - 1]
        far = swap(jnp.where(parity, bottom, top), "gz", 1)
        near = swap(jnp.where(parity, top, bottom), "gz", 0)
        return [near, far]

    sizes = {
        stage: len(columns_of(stage)) * len(slot_blocks(stage, leaves)) for stage in STAGES
    }
    tile_counts = {
        stage: len(columns_of(stage)) * len(slots_of(stage, leaves)) for stage in STAGES
    }
    acc_shape = jax.ShapeDtypeStruct((leaves, 48, per_leaf), f32)
    acc_scratch = pltpu.VMEM((leaves, 48, per_leaf), f32)
    right_shapes = [
        jax.ShapeDtypeStruct((sizes[stage], 48, per_leaf), bf16) for stage in STAGES
    ]

    def tile_scratch(stage):
        return pltpu.VMEM((tile_counts[stage], 8, per_leaf), f32)

    def weight_scratch(stage):
        return pltpu.VMEM((sizes[stage], 8, per_leaf), f32)

    def call(body, name, operands, out, scratch, size, ops):
        return pl.pallas_call(
            body,
            out_shape=out,
            in_specs=[vmem] * len(operands),
            out_specs=[vmem] * len(out),
            scratch_shapes=scratch,
            compiler_params=params,
            cost_estimate=cost(size, ops),
            name=name,
        )(*operands)

    def moment_call(stage, sources, right=None, acc=None):
        size = sizes[stage]
        out = [
            acc_shape,
            jax.ShapeDtypeStruct((size, 2 * per_leaf, per_leaf), bf16),
            jax.ShapeDtypeStruct((size, per_leaf, per_leaf), f32),
        ]
        scratch = [tile_scratch(stage), weight_scratch(stage)]
        operands = [own] + list(sources)
        if stage == "own":
            body = functools.partial(moment_own_kernel, leaves, per_leaf)
            out += right_shapes
        elif stage == "z":
            body = functools.partial(field_kernel, leaves, per_leaf, len(sources))
            operands += [right, acc, extra]
            out[0] = jax.ShapeDtypeStruct((leaves, 8, per_leaf), f32)
            scratch += [acc_scratch]
        else:
            body = functools.partial(moment_kernel, stage, leaves, per_leaf, len(sources))
            operands += [right, acc]
        return call(body, "moments_" + stage, operands, out, scratch, size, 55)

    def force_call(stage, sources, places, right, accs, kept, fields):
        size = sizes[stage]
        out = [acc_shape] * 2
        scratch = [tile_scratch(stage)] * 2 + [weight_scratch(stage)]
        operands = [own] + list(sources) + list(places)
        if stage == "own":
            body = functools.partial(force_own_kernel, leaves, per_leaf)
            operands += [fields] + list(kept)
            out += right_shapes
        elif stage == "z":
            body = functools.partial(finish_kernel, leaves, per_leaf, len(sources))
            operands += [right] + list(accs) + list(kept) + [fields]
            out = [
                jax.ShapeDtypeStruct((1, 1, 3, leaves, per_leaf), f32),
                jax.ShapeDtypeStruct((1, 1, leaves, per_leaf), f32),
            ]
            scratch += [acc_scratch] * 2
        else:
            body = functools.partial(force_kernel, stage, leaves, per_leaf, len(sources))
            operands += [right] + list(accs) + list(kept)
        return call(body, "force_" + stage, operands, out, scratch, size, 36)

    from_y = exchange_y(own)
    acc, w_own, g_own, *rights = moment_call("own", [])
    from_y, acc = lax.optimization_barrier((from_y, acc))
    from_x = exchange_x(own, from_y)
    acc, *kept_y = moment_call("y", from_y, rights[1], acc)
    from_x, acc = lax.optimization_barrier((from_x, acc))
    from_z = exchange_z(own, from_y, from_x)
    acc, *kept_x = moment_call("x", from_x, rights[2], acc)
    fields, *kept_z = moment_call("z", from_z, rights[3], acc)

    field_y = exchange_y(fields)
    *accs, _, right_y, right_x, right_z = force_call(
        "own", [], [], None, None, (w_own, g_own), fields
    )
    field_y, accs = lax.optimization_barrier((field_y, accs))
    field_x = exchange_x(fields, field_y)
    accs = force_call("y", field_y, from_y, right_y, accs, kept_y, fields)
    field_x, accs = lax.optimization_barrier((field_x, accs))
    field_z = exchange_z(fields, field_y, field_x)
    accs = force_call("x", field_x, from_x, right_x, accs, kept_x, fields)
    acceleration, heating = force_call("z", field_z, from_z, right_z, accs, kept_z, fields)
    return (jnp.swapaxes(acceleration, 2, 3), heating)


def solution(mesh):
    in_specs = (
        P("gx", "gy", "gz", None, None),
        P("gx", "gy", "gz", None, None),
        P("gx", "gy", "gz", None),
        P("gx", "gy", "gz", None),
        P("gx", "gy", "gz", None),
        P("gx", "gy", "gz", None),
        P("gx", "gy", "gz", None),
        P("gx", "gy", "gz"),
    )
    out_specs = (P("gx", "gy", "gz", None, None), P("gx", "gy", "gz", None))
    return jax.shard_map(
        per_device, mesh=mesh, in_specs=in_specs, out_specs=out_specs, check_vma=False
    )
```

```python
import functools
import math

import jax
import jax.numpy as jnp
from jax import lax
from jax.experimental import pallas as pl
from jax.experimental.pallas import tpu as pltpu
from jax.sharding import PartitionSpec as P


kernel_norm = 21.0 / (16.0 * math.pi)
pressure_factor = 2.0 / 3.0
ridge_factor = 0.1
pair_scale = -160.0 * kernel_norm

LIMIT = 16 * 1024 * 1024
PACK_LIMIT = 63 * 1024 * 1024 - 65536
X, _, _, H, V, M, FLAGS = range(7)
VX, _, VZ, PR, CA, _, _, _ = range(8)


def code_of(step):
    index = (step[0] + 1) * 9 + (step[1] + 1) * 3 + step[2] + 1
    return index if index < 13 else index - 1


def swap(array, axis, phase):
    count = lax.axis_size(axis)
    pairs = []
    for first in range(phase, count, 2):
        second = (first + 1) % count
        pairs += [(first, second), (second, first)]
    return lax.ppermute(array, axis, pairs)


def swaps(array, axis):
    if lax.axis_size(axis) == 2:
        return [swap(array, axis, 0)]
    results = []
    for phase in (1, 0):
        results.append(swap(array, axis, phase))
    return results[::-1]


def beside(get, step, axis):
    if step == 0:
        return get(0)
    if lax.axis_size(axis) == 2:
        return get(1)
    even = lax.axis_index(axis) % 2 == 0
    first, second = (1, 2) if step == 1 else (2, 1)
    return jnp.where(even, get(first), get(second))


def split(values, parts):
    pieces = []
    for _ in range(parts - 1):
        piece = values.astype(jnp.bfloat16).astype(jnp.float32)
        pieces.append(piece)
        values = values - piece
    return pieces + [values]


def stacked(parts):
    return jnp.concatenate(parts, axis=0).astype(jnp.bfloat16)


def left_form(features):
    high, middle, low = split(features, 3)
    return stacked([high, high, middle, high, low, middle]).T


def right_form(features):
    high, middle, low = split(features, 3)
    return stacked([high, middle, high, low, high, middle])


def pair_matrix(values):
    return jnp.concatenate(split(values, 2), axis=0).astype(jnp.bfloat16)


def feature_rows(first, second):
    pieces = [piece for pair in zip(split(first, 3), split(second, 3)) for piece in pair]
    rows = stacked(pieces)
    return jnp.concatenate([rows, rows], axis=1)


def dot(left, right):
    return jnp.dot(left, right, preferred_element_type=jnp.float32)


def row_index(per_leaf):
    return lax.broadcasted_iota(jnp.int32, (8, per_leaf), 0)


def chosen(pairs, other):
    for condition, value in pairs[::-1]:
        other = jnp.where(condition, value, other)
    return other


def front_sum(tile, row):
    return jnp.sum(jnp.where(row < 3, tile, 0.0), axis=0, keepdims=True)


def at_front(row, values):
    x, y, z = values
    return chosen([(row == 0, x), (row == 1, y), (row == 2, z)], 0.0)


def rows_of(tile, first, count=1):
    return [tile[k : k + 1] for k in range(first, first + count)]


STAGES = ("own", "y", "x", "z")


def columns_of(stage):
    return {"own": (0,), "y": (0,), "x": (-1, 1), "z": (-1, 0, 1)}[stage]


def stage_of(dx, dy, outside):
    if dx == 0 and dy == 0 and not outside:
        return "own"
    if dy and outside:
        return "z"
    return "x" if dx else "y"


def slots_of(stage, leaves):
    slots = {}
    column = columns_of(stage)[0]
    for dy in (-1, 0, 1):
        for leaf in range(leaves):
            for level in range(leaf - 1, leaf + 2):
                outside = level < 0 or level >= leaves
                if stage_of(column, dy, outside) == stage:
                    key = (abs(dy) if lax.axis_size("gy") == 2 else dy, level)
                    slots.setdefault(key, []).append((leaf, dy))
    return list(slots.items())


def chunks_of(stage, leaves):
    chunks = []
    first = 0
    for k, ((_, level), blocks) in enumerate(slots_of(stage, leaves)):
        for start in range(0, len(blocks), 2):
            chunks.append((k, level, first + start, blocks[start : start + 2]))
        first += len(blocks)
    return chunks


def block_count(stage, leaves):
    return sum(len(blocks) for _, blocks in slots_of(stage, leaves))


def lanes(first, count, per_leaf):
    return slice(first * per_leaf, (first + count) * per_leaf)


def tile_at(refs, stage, dx, dy, level, leaves):
    ny = 1 if lax.axis_size("gy") == 2 else 2
    outside = level < 0 or level >= leaves

    def along_z(get):
        if not outside:
            return get(level)
        even = lax.axis_index("gz") % 2 == 0
        near, far = get(0), get(1)
        return jnp.where(even, near, far) if level >= leaves else jnp.where(even, far, near)

    def along_x(kx):
        def along_y(ky):
            if stage == "own":
                return refs[0][level]
            if stage == "y":
                return along_z(lambda k: refs[ny + k][0] if outside else refs[ky - 1][k])
            if stage == "x":
                base = leaves * (1 + ny if outside else ky)
                return along_z(lambda k: refs[kx - 1][base + k])
            return along_z(lambda k: refs[ky - 1][2 * kx + k])

        return beside(along_y, dy, "gy")

    return beside(along_x, dx, "gx")


def place_shift(dx, dy, level, leaves):
    return (dx, float(dy), float(level) - 0.5 * (leaves - 1))


def centred(tile, row):
    return tile - jnp.where(row < 3, 0.5, 0.0)


def gather_tiles(tiles, sources, stage, leaves):
    slots = slots_of(stage, leaves)
    for column, dx in enumerate(columns_of(stage)):
        for k, ((dy, level), _) in enumerate(slots):
            tiles[column * len(slots) + k] = tile_at(sources, stage, dx, dy, level, leaves)


def find_weights(weights, own, tiles, stage, leaves, per_leaf):
    slots = slots_of(stage, leaves)
    for column, dx in enumerate(columns_of(stage)):
        first = 0
        for k, ((_, level), blocks) in enumerate(slots):
            for leaf, dy in blocks:
                step = (dx, dy, level - leaf)
                if step == (0, 0, 0):
                    weight = jnp.ones((1, 1), jnp.float32)
                else:
                    code = code_of(step)
                    tile = tiles[column * len(slots) + k]
                    weight = (
                        own[leaf][FLAGS : FLAGS + 1, code : code + 1]
                        + tile[FLAGS : FLAGS + 1, 25 - code : 26 - code]
                    )
                weights[column, :, lanes(first, 1, per_leaf)] = jnp.broadcast_to(
                    weight, (8, per_leaf)
                )
                first += 1


def add_weighted(acc, leaf, count, per_leaf, sums, weight):
    where = lanes(leaf, count, per_leaf)
    for k in range(6):
        part = slice(8 * k, 8 * k + 8)
        acc[part, where] = acc[part, where] + sums[part] * weight


def runs_of(blocks):
    runs = []
    for at, (leaf, dy) in enumerate(blocks):
        if runs:
            start, count = runs[-1]
            if blocks[start][1] == dy and blocks[start][0] + count == leaf:
                runs[-1] = (start, count + 1)
                continue
        runs.append((at, 1))
    return runs


def over_columns(stage, step_fn):
    columns = columns_of(stage)
    if len(columns) == 1:
        step_fn(0, float(columns[0]))
        return
    pace = columns[1] - columns[0]

    def body(column, carry):
        step_fn(column, (column * pace + columns[0]).astype(jnp.float32))
        return carry

    lax.fori_loop(0, len(columns), body, 0)


def each_right(leaves, per_leaf, rights, form):
    for stage, right in zip(STAGES, rights):
        for column, dx in enumerate(columns_of(stage)):
            for _, level, first, blocks in chunks_of(stage, leaves):
                for at, (leaf, dy) in enumerate(blocks):
                    shift = (0.5 + dx, 0.5 + dy, 0.5 + level - leaf)
                    right[column, :, lanes(first + at, 1, per_leaf)] = right_form(
                        form(leaf, shift)
                    )


def moment_rights(own, leaves, per_leaf, rights):
    row = row_index(per_leaf)

    def form(leaf, shift):
        spot = own[leaf] - at_front(row, shift)
        far = front_sum(spot * spot, row)
        return chosen([(row < 3, -2.0 * spot), (row == 4, 1.0), (row == 5, far)], 0.0)

    each_right(leaves, per_leaf, rights, form)


def moment_body(stage, leaves, per_leaf, own, sources, right, acc, w_out, g_out, tiles, weights):
    row = row_index(per_leaf)
    gather_tiles(tiles, sources, stage, leaves)
    find_weights(weights, own, tiles, stage, leaves, per_leaf)
    widths = [
        right_form(chosen([(row == 3, 1.0), (row == 5, own[leaf][H : H + 1])], 0.0))
        for leaf in range(leaves)
    ]
    slots = slots_of(stage, leaves)

    def step_fn(column, dx):
        state = {}
        for k, level, first, blocks in chunks_of(stage, leaves):
            tile = tiles[column * len(slots) + k]
            spot = centred(tile, row)
            here = lanes(first, len(blocks), per_leaf)
            if k not in state:
                near = front_sum(spot * spot, row)
                left = left_form(
                    chosen([(row < 4, spot), (row == 4, near), (row == 5, 1.0)], 0.0)
                )
                users = sorted({leaf for leaf, _ in slots[k][1]})
                width = jnp.concatenate([widths[leaf] for leaf in users], axis=1)
                sizes = dot(left, width)
                inverses = {
                    leaf: 1.0 / sizes[:, lanes(at, 1, per_leaf)] for at, leaf in enumerate(users)
                }
                squares = {leaf: value * value for leaf, value in inverses.items()}
                cubes = {leaf: squares[leaf] * value for leaf, value in inverses.items()}
                state[k] = left, inverses, squares, cubes, {}
            left, inverses, squares, cubes, features = state[k]
            volume, mass = tile[V : V + 1], tile[M : M + 1]
            for _, dy in blocks:
                if dy not in features:
                    x, y, z = [
                        part + shift
                        for part, shift in zip(
                            rows_of(spot, X, 3), place_shift(dx, dy, level, leaves)
                        )
                    ]
                    front = chosen(
                        [(row == 0, 1.0), ((row == 2) | (row == 7), y), (row == 3, z)], x
                    ) * chosen([(row < 4, 1.0), (row == 4, x), (row == 6, z)], y)
                    back = chosen([(row == 0, y), (row == 1, z)], 1.0) * jnp.where(row < 2, z, 1.0)
                    features[dy] = feature_rows(
                        front * volume,
                        back * chosen([(row < 2, volume), (row == 2, mass)], 0.0),
                    )

            def wide(values):
                return jnp.concatenate([values[leaf] for leaf, _ in blocks], axis=1)

            dist_sq = jnp.maximum(dot(left, right[column, :, here]), 1e-30)
            dist = dist_sq * lax.rsqrt(dist_sq)
            remain = jnp.maximum(1.0 - dist * wide(inverses), 0.0)
            edge = wide(cubes) * (remain * remain * remain)
            pair_w = pair_matrix(edge * (remain * (remain - 1.25)))
            w_out[column, :, here] = pair_w
            g_out[column, :, here] = edge * wide(squares)
            for start, count in runs_of(blocks):
                leaf, dy = blocks[start]
                sums = dot(features[dy], pair_w[:, lanes(start, count, per_leaf)])
                weight = weights[column, :, lanes(first + start, count, per_leaf)]
                add_weighted(acc, leaf, count, per_leaf, sums, weight)

    over_columns(stage, step_fn)


def moment_own_kernel(leaves, per_leaf, own, acc, w_out, g_out, *refs):
    rights, (tiles, weights) = refs[:4], refs[4:]
    acc[...] = jnp.zeros_like(acc)
    moment_rights(own, leaves, per_leaf, rights)
    moment_body(
        "own", leaves, per_leaf, own, (own,), rights[0], acc, w_out, g_out, tiles, weights
    )


def moment_kernel(stage, leaves, per_leaf, count, *refs):
    own, sources = refs[0], refs[1 : 1 + count]
    right, acc_in, acc, w_out, g_out, tiles, weights = refs[1 + count :]
    acc[...] = acc_in[...]
    moment_body(
        stage, leaves, per_leaf, own, sources, right, acc, w_out, g_out, tiles, weights
    )


def corrections(moments, smooth, energy):
    density, zeroth, first_x, first_y, first_z, s_xx, s_xy, s_xz, s_yy, s_yz, s_zz = moments
    ridge_term = ridge_factor * smooth * smooth * zeroth
    s_xx = s_xx + ridge_term
    s_yy = s_yy + ridge_term
    s_zz = s_zz + ridge_term
    c_xx = s_yy * s_zz - s_yz * s_yz
    c_xy = s_yz * s_xz - s_xy * s_zz
    c_xz = s_xy * s_yz - s_yy * s_xz
    c_yy = s_xx * s_zz - s_xz * s_xz
    c_yz = s_xy * s_xz - s_xx * s_yz
    c_zz = s_xx * s_yy - s_xy * s_xy
    determinant = s_xx * c_xx + s_xy * c_xy + s_xz * c_xz
    solve_x = (c_xx * first_x + c_xy * first_y + c_xz * first_z) / determinant
    solve_y = (c_xy * first_x + c_yy * first_y + c_yz * first_z) / determinant
    solve_z = (c_xz * first_x + c_yz * first_y + c_zz * first_z) / determinant
    coef_a = 1.0 / (zeroth - (first_x * solve_x + first_y * solve_y + first_z * solve_z))
    pressure = pressure_factor * density * energy
    return [pressure, coef_a, -coef_a * solve_x, -coef_a * solve_y, -coef_a * solve_z]


def gathered(acc, leaf, per_leaf):
    sums = acc[:, lanes(leaf, 1, per_leaf)]
    return sums[0:16] + (sums[16:32] + sums[32:48])


def own_place(tile, leaf, leaves):
    shift = place_shift(0.0, 0, leaf, leaves)
    return [part + (move - 0.5) for part, move in zip(rows_of(tile, X, 3), shift)]


def field_kernel(leaves, per_leaf, count, *refs):
    own, sources = refs[0], refs[1 : 1 + count]
    right, acc_in, extra, fields_out, w_out, g_out, tiles, weights, acc = refs[1 + count :]
    acc[...] = acc_in[...]
    moment_body("z", leaves, per_leaf, own, sources, right, acc, w_out, g_out, tiles, weights)
    columns = []
    for leaf in range(leaves):
        sums = gathered(acc, leaf, per_leaf)
        zeroth, fx, fy, fz, sxx, sxy, sxz, syy, syz, szz, density = rows_of(sums, 0, 11)
        x, y, z = own_place(own[leaf], leaf, leaves)
        mx, my, mz = x * zeroth - fx, y * zeroth - fy, z * zeroth - fz
        columns.append(
            [
                density,
                zeroth,
                mx,
                my,
                mz,
                x * mx - x * fx + sxx,
                x * my - y * fx + sxy,
                x * mz - z * fx + sxz,
                y * my - y * fy + syy,
                y * mz - z * fy + syz,
                z * mz - z * fz + szz,
                own[leaf][H : H + 1],
                extra[leaf][3:4],
            ]
        )
    rows = [jnp.concatenate(parts, axis=0) for parts in zip(*columns)]
    fields = corrections([0.2 * part for part in rows[:11]], rows[11], rows[12])
    for leaf in range(leaves):
        fields_out[leaf, VX : VZ + 1, :] = extra[leaf][0:3]
        for k, value in enumerate(fields):
            fields_out[leaf, PR + k : PR + k + 1, :] = value[leaf : leaf + 1]


def force_rights(own, fields, leaves, per_leaf, rights):
    row = row_index(per_leaf)

    def form(leaf, shift):
        spot = own[leaf] - at_front(row, shift)
        coefs = pltpu.roll(fields[leaf], 3, 0)
        full = fields[leaf][CA : CA + 1] + front_sum(coefs * spot, row)
        return chosen(
            [(row < 3, -coefs), (row == 3, full), (row == 4, 1.0)], -pltpu.roll(spot, 5, 0)
        )

    each_right(leaves, per_leaf, rights, form)


def force_body(stage, leaves, per_leaf, own, sources, places, right, accs, w_in, g_in, scratch):
    row = row_index(per_leaf)
    tiles, field_tiles, weights = scratch
    acc_w, acc_g = accs
    gather_tiles(tiles, places, stage, leaves)
    gather_tiles(field_tiles, sources, stage, leaves)
    find_weights(weights, own, tiles, stage, leaves, per_leaf)
    slots = slots_of(stage, leaves)

    def step_fn(column, dx):
        state = {}
        for k, level, first, blocks in chunks_of(stage, leaves):
            tile = tiles[column * len(slots) + k]
            field = field_tiles[column * len(slots) + k]
            spot = centred(tile, row)
            here = lanes(first, len(blocks), per_leaf)
            volume, pressure = tile[V : V + 1], field[PR : PR + 1]

            def weighted(front, back, factor):
                rows = (factor * volume) * chosen(
                    [
                        (row < 3, field),
                        (row == 3, 1.0),
                        (row == 4, front_sum(front * field, row)),
                    ],
                    back,
                )
                return feature_rows(rows, pressure * rows)

            if k not in state:
                coefs = pltpu.roll(field, 3, 0)
                full = field[CA : CA + 1] + front_sum(coefs * spot, row)
                left = left_form(
                    chosen([(row < 3, spot), (row == 3, 1.0), (row == 4, full)], field)
                )
                state[k] = left, weighted(coefs, field, 0.2), {}
            left, with_w, with_g = state[k]
            for _, dy in blocks:
                if dy not in with_g:
                    front = spot + at_front(row, place_shift(dx, dy, level, leaves))
                    with_g[dy] = weighted(front, pltpu.roll(front, 5, 0), 1.0)
            radial = pair_matrix(g_in[column, :, here] * dot(left, right[column, :, here]))
            sums_w = dot(with_w, w_in[column, :, here])
            for start, count in runs_of(blocks):
                leaf, dy = blocks[start]
                part = lanes(start, count, per_leaf)
                weight = weights[column, :, lanes(first + start, count, per_leaf)]
                add_weighted(acc_w, leaf, count, per_leaf, sums_w[:, part], weight)
                sums_g = dot(with_g[dy], radial[:, part])
                add_weighted(acc_g, leaf, count, per_leaf, sums_g, weight)

    over_columns(stage, step_fn)


def force_own_kernel(leaves, per_leaf, own, fields, w_in, g_in, acc_w, acc_g, *refs):
    rights, scratch = refs[:4], refs[4:]
    acc_w[...] = jnp.zeros_like(acc_w)
    acc_g[...] = jnp.zeros_like(acc_g)
    force_rights(own, fields, leaves, per_leaf, rights)
    force_body(
        "own",
        leaves,
        per_leaf,
        own,
        (fields,),
        (own,),
        rights[0],
        (acc_w, acc_g),
        w_in,
        g_in,
        scratch,
    )


def force_kernel(stage, leaves, per_leaf, count, *refs):
    own, sources, places = refs[0], refs[1 : 1 + count], refs[1 + count : 1 + 2 * count]
    right, w_before, g_before, w_in, g_in, acc_w, acc_g, *scratch = refs[1 + 2 * count :]
    acc_w[...] = w_before[...]
    acc_g[...] = g_before[...]
    accs = (acc_w, acc_g)
    force_body(
        stage, leaves, per_leaf, own, sources, places, right, accs, w_in, g_in, scratch
    )


def finish_kernel(leaves, per_leaf, count, *refs):
    own, sources, places = refs[0], refs[1 : 1 + count], refs[1 + count : 1 + 2 * count]
    rest = refs[1 + 2 * count :]
    right, w_before, g_before, w_in, g_in, fields, acceleration, heating = rest[:8]
    scratch, accs = rest[8:11], rest[11:13]
    accs[0][...] = w_before[...]
    accs[1][...] = g_before[...]
    force_body("z", leaves, per_leaf, own, sources, places, right, accs, w_in, g_in, scratch)
    for leaf in range(leaves):
        tile = own[leaf]
        vx, vy, vz, pressure, _, cx, cy, cz = rows_of(fields[leaf], 0, 8)
        sums_w, sums_g = [gathered(acc, leaf, per_leaf) for acc in accs]
        w_rows = rows_of(pressure * sums_w[0:8] + sums_w[8:16], 0, 8)
        g_rows = rows_of(pressure * sums_g[0:8] + sums_g[8:16], 0, 8)
        spots = own_place(tile, leaf, leaves)
        ratio = tile[V : V + 1] / tile[M : M + 1]
        work = w_rows[4] + g_rows[4]
        for k, (coef, spot, speed) in enumerate(zip((cx, cy, cz), spots, (vx, vy, vz))):
            force = (coef * w_rows[3] - w_rows[5 + k]) + (spot * g_rows[3] - g_rows[5 + k])
            work = work + speed * force - coef * w_rows[k] - spot * g_rows[k]
            acceleration[0, 0, k, leaf : leaf + 1, :] = (-0.5 * ratio) * force
        heating[0, 0, leaf : leaf + 1, :] = (0.25 * ratio) * work


def pack_kernel(leaves, per_leaf, *refs):
    inputs, out, extra, held, sems = refs[:8], refs[8], refs[9], refs[10:18], refs[18]
    neighbours, counts = held[6:8]
    copies = [
        pltpu.make_async_copy(source, target, sems.at[k])
        for k, (source, target) in enumerate(zip(inputs, held))
    ]
    for copy in copies[::-1]:
        copy.start()
    for copy in copies[6:]:
        copy.wait()
    lane = lax.broadcasted_iota(jnp.int32, (1, per_leaf), 1)
    for leaf in range(leaves):
        flags = jnp.zeros((1, per_leaf), jnp.float32)
        for slot in range(neighbours.shape[3]):
            code = jnp.where(slot < counts[0, 0, leaf], neighbours[0, 0, leaf, slot], -1)
            flags = flags + jnp.where(lane == code, 1.0, 0.0)
        out[leaf, FLAGS : FLAGS + 1, :] = flags
        out[leaf, FLAGS + 1 : FLAGS + 2, :] = jnp.zeros((1, per_leaf), jnp.float32)
        extra[leaf, 4:8, :] = jnp.zeros((4, per_leaf), jnp.float32)
    for copy in copies[:6]:
        copy.wait()
    offsets, velocity, masses, volumes, energies, smoothing = held[:6]
    for leaf in range(leaves):
        one = slice(leaf, leaf + 1)
        for part in range(3):
            out[leaf, part : part + 1, :] = offsets[0, 0, part, one]
            extra[leaf, part : part + 1, :] = velocity[0, 0, part, one]
        out[leaf, H : H + 1, :] = smoothing[0, 0, one]
        out[leaf, V : V + 1, :] = pair_scale * volumes[0, 0, one]
        out[leaf, M : M + 1, :] = pair_scale * masses[0, 0, one]
        extra[leaf, 3:4, :] = energies[0, 0, one]


def per_device(offsets, velocity, masses, volumes, energies, smoothing, neighbours, counts):
    leaves, per_leaf = masses.shape[2], masses.shape[3]
    f32, bf16 = jnp.float32, jnp.bfloat16
    vmem = pl.BlockSpec(memory_space=pltpu.VMEM)
    hbm = pl.BlockSpec(memory_space=pltpu.HBM)
    params = pltpu.CompilerParams(vmem_limit_bytes=LIMIT)
    parity = lax.axis_index("gz") % 2 == 0
    offsets = jnp.swapaxes(offsets, 2, 3)
    velocity = jnp.swapaxes(velocity, 2, 3)

    def cost(blocks, ops):
        return pl.CostEstimate(
            flops=blocks * per_leaf * per_leaf * ops, bytes_accessed=blocks * 4096, transcendentals=0
        )

    inputs = (offsets, velocity, masses, volumes, energies, smoothing)
    own, extra = pl.pallas_call(
        functools.partial(pack_kernel, leaves, per_leaf),
        out_shape=[pltpu.VMEM((leaves, 8, per_leaf), f32)] * 2,
        in_specs=[hbm] * 8,
        out_specs=[vmem] * 2,
        scratch_shapes=[pltpu.VMEM(array.shape, f32) for array in inputs]
        + [pltpu.SMEM(array.shape, jnp.int32) for array in (neighbours, counts)]
        + [pltpu.SemaphoreType.DMA((8,))],
        compiler_params=pltpu.CompilerParams(vmem_limit_bytes=PACK_LIMIT),
        name="pack",
    )(*inputs, neighbours, counts)

    def exchange_first(tile):
        bottom, top = tile[0:1], tile[leaves - 1 : leaves]
        far = swap(jnp.where(parity, bottom, top), "gz", 1)
        near = swap(jnp.where(parity, top, bottom), "gz", 0)
        return swaps(tile, "gy"), [near, far]

    def exchange_x(tile, from_y, from_z):
        return swaps(jnp.concatenate([tile] + from_y + from_z, axis=0), "gx")

    def exchange_last(from_z, from_x):
        ends = [array[-2:] for array in from_x]
        return swaps(jnp.concatenate(from_z + ends, axis=0), "gy")

    counts_of = {stage: block_count(stage, leaves) for stage in STAGES}
    tile_counts = {
        stage: len(columns_of(stage)) * len(slots_of(stage, leaves)) for stage in STAGES
    }
    acc_shape = jax.ShapeDtypeStruct((48, leaves * per_leaf), f32)
    acc_scratch = pltpu.VMEM((48, leaves * per_leaf), f32)

    def pair_shape(stage, rows, dtype):
        return (len(columns_of(stage)), rows, counts_of[stage] * per_leaf), dtype

    right_shapes = [jax.ShapeDtypeStruct(*pair_shape(stage, 48, bf16)) for stage in STAGES]

    def tile_scratch(stage):
        return pltpu.VMEM((tile_counts[stage], 8, per_leaf), f32)

    def weight_scratch(stage):
        return pltpu.VMEM(*pair_shape(stage, 8, f32))

    def call(body, operands, out, scratch, size, ops):
        return pl.pallas_call(
            body,
            out_shape=out,
            in_specs=[vmem] * len(operands),
            out_specs=[vmem] * len(out),
            scratch_shapes=scratch,
            compiler_params=params,
            cost_estimate=cost(size, ops),
        )(*operands)

    def moment_call(stage, sources, right=None, acc=None):
        size = len(columns_of(stage)) * counts_of[stage]
        out = [
            acc_shape,
            jax.ShapeDtypeStruct(*pair_shape(stage, 2 * per_leaf, bf16)),
            jax.ShapeDtypeStruct(*pair_shape(stage, per_leaf, f32)),
        ]
        scratch = [tile_scratch(stage), weight_scratch(stage)]
        operands = [own] + list(sources)
        if stage == "own":
            body = functools.partial(moment_own_kernel, leaves, per_leaf)
            out += right_shapes
        elif stage == "z":
            body = functools.partial(field_kernel, leaves, per_leaf, len(sources))
            operands += [right, acc, extra]
            out[0] = jax.ShapeDtypeStruct((leaves, 8, per_leaf), f32)
            scratch += [acc_scratch]
        else:
            body = functools.partial(moment_kernel, stage, leaves, per_leaf, len(sources))
            operands += [right, acc]
        return call(body, operands, out, scratch, size, 55)

    def force_call(stage, sources, places, right, accs, kept, fields):
        size = len(columns_of(stage)) * counts_of[stage]
        out = [acc_shape] * 2
        scratch = [tile_scratch(stage)] * 2 + [weight_scratch(stage)]
        operands = [own] + list(sources) + list(places)
        if stage == "own":
            body = functools.partial(force_own_kernel, leaves, per_leaf)
            operands += [fields] + list(kept)
            out += right_shapes
        elif stage == "z":
            body = functools.partial(finish_kernel, leaves, per_leaf, len(sources))
            operands += [right] + list(accs) + list(kept) + [fields]
            out = [
                jax.ShapeDtypeStruct((1, 1, 3, leaves, per_leaf), f32),
                jax.ShapeDtypeStruct((1, 1, leaves, per_leaf), f32),
            ]
            scratch += [acc_scratch] * 2
        else:
            body = functools.partial(force_kernel, stage, leaves, per_leaf, len(sources))
            operands += [right] + list(accs) + list(kept)
        return call(body, operands, out, scratch, size, 36)

    from_y, from_z = exchange_first(own)
    acc, w_own, g_own, *rights = moment_call("own", [])
    from_y, from_z, acc = lax.optimization_barrier((from_y, from_z, acc))
    from_x = exchange_x(own, from_y, from_z)
    acc, *kept_y = moment_call("y", from_y + from_z, rights[1], acc)
    from_x, acc = lax.optimization_barrier((from_x, acc))
    from_last = exchange_last(from_z, from_x)
    acc, *kept_x = moment_call("x", from_x, rights[2], acc)
    fields, *kept_z = moment_call("z", from_last, rights[3], acc)

    field_y, field_z = exchange_first(fields)
    *accs, _, right_y, right_x, right_z = force_call(
        "own", [], [], None, None, (w_own, g_own), fields
    )
    field_y, field_z, accs = lax.optimization_barrier((field_y, field_z, accs))
    field_x = exchange_x(fields, field_y, field_z)
    accs = force_call(
        "y", field_y + field_z, from_y + from_z, right_y, accs, kept_y, fields
    )
    field_x, accs = lax.optimization_barrier((field_x, accs))
    field_last = exchange_last(field_z, field_x)
    accs = force_call("x", field_x, from_x, right_x, accs, kept_x, fields)
    acceleration, heating = force_call("z", field_last, from_last, right_z, accs, kept_z, fields)
    return (jnp.swapaxes(acceleration, 2, 3), heating)


def solution(mesh):
    in_specs = (
        P("gx", "gy", "gz", None, None),
        P("gx", "gy", "gz", None, None),
        P("gx", "gy", "gz", None),
        P("gx", "gy", "gz", None),
        P("gx", "gy", "gz", None),
        P("gx", "gy", "gz", None),
        P("gx", "gy", "gz", None),
        P("gx", "gy", "gz"),
    )
    out_specs = (P("gx", "gy", "gz", None, None), P("gx", "gy", "gz", None))
    return jax.shard_map(
        per_device, mesh=mesh, in_specs=in_specs, out_specs=out_specs, check_vma=False
    )
```
